32 devices in a mesh: groups: 2 (over x), lines: 16 (over z, y, core).
Axes of the slice: x: 2, y: 2, z: 4, core: 2. Of those that a mesh axis runs over, the one named last changes fastest.
Arguments:
- raw_echo: bfloat16 [8, 2, 2048, 512], P('groups', None, 'lines'), parts along dimension 0, may hold values from -6 to 6
- range_filter: bfloat16 [2, 512, 512], replicated, may hold values from -0.1875 to 0.1875
- azimuth_phase: float32 [512, 2048], P('lines'), may hold values from -3.140625 to 3.140625
- pair_offset: int32 [4], replicated, may hold values from 1 to 3
Outputs:
- filtered: float32 [8, 2, 128, 1024], P('groups', None, None, 'lines'), parts along dimension 0
The draws below stay inside these ranges and needn't reach their ends.
There are 2 independent parts, one for each index of `groups`. The reference program is written for one: setup_inputs(seed, part) draws one part's arguments, and reference() takes and returns one part's arrays. A program takes and returns all parts, laid end to end along the dimension named above; an argument that names none is the same for every part. Nothing has to cross between parts.
Inputs may be any that keep to these rules, and one draw needn't show every extreme that they name: Date d is paired with date (d + pair_offset[d]) mod 4.
All inputs are finite; a program needn't handle non-finite values.
Results may differ from the reference program's by a relative error of at most 0.0095.
Values may be sent and summed in bfloat16 or wider, within the bound.
A program may use at most 192 MiB of HBM per device.

```python
import jax
import jax.numpy as jnp
from jax import lax

DATES = 4
GATES = 512
ML_RG = 4
ML_AZ = 2
PATCH = 32
LINES = 2048


def touch_ends(drawn, own_key, low, largest):
    longest = drawn.shape.index(max(drawn.shape))
    spots = []
    for shift in (0, 1):
        where = [jax.random.randint(jax.random.fold_in(own_key, axis), (), 0, length) for axis, length in enumerate(drawn.shape)]
        where[longest] = (where[longest] + shift) % drawn.shape[longest]
        spots.append(tuple(where))
    return drawn.at[spots[0]].set(low).at[spots[1]].set(largest)


def steps_of(stream_key, shape, cuts, low, top_value):
    def one(dim, blocks):
        steps = jax.random.uniform(jax.random.fold_in(jax.random.fold_in(stream_key, 6), dim), (blocks,), jnp.float32, low / len(cuts), top_value / len(cuts))
        return jnp.repeat(jnp.exp(steps), shape[dim] // blocks).reshape((-1,) + (1,) * (len(shape) - dim - 1))

    factor_of = one(*cuts[0])
    for cut in cuts[1:]:
        factor_of = factor_of * one(*cut)
    return factor_of


def scatter_about(key, extent, width, bound, split=(), held_as=jnp.bfloat16):
    loudness = steps_of(key, extent, split, -0.22, 0.18) if split else 1.0
    values = jax.random.normal(key, extent, jnp.float32) * width * loudness
    return jnp.minimum(jnp.maximum(values, -bound), bound).astype(held_as)


def setup_inputs(seed: int = 0, part: int = 0) -> dict:
    key_list = jax.random.split(jax.random.key(seed), 5)
    own_keys = jax.random.split(jax.random.fold_in(key_list[4], part), 5)
    return {
        "raw_echo": scatter_about(own_keys[0], (DATES, 2, LINES, GATES), 1.0, 6.0, ((2, 16),)),
        "range_filter": scatter_about(key_list[1], (2, GATES, GATES), (2 * GATES) ** -0.5, 0.1875),
        "azimuth_phase": jnp.clip(jax.random.uniform(key_list[2], (GATES, LINES), jnp.float32, -3.140625, 3.140625), -3.140625, 3.140625),
        "pair_offset": touch_ends(jax.random.randint(key_list[3], (DATES,), 1, DATES), jax.random.fold_in(key_list[3], 1), 1, DATES - 1).astype(jnp.int32),
    }


PRECISION_MAX = lax.Precision.HIGHEST
BOX_FLOOR = 0.25

def compress(raw_echo, range_filter):
    w_real = jnp.stack([range_filter[0], -range_filter[1]])
    w_imag = jnp.stack([range_filter[1], range_filter[0]])
    stacked = jnp.stack([w_real, w_imag]).astype(jnp.float32)
    result = jnp.einsum('ecog,dclg->deol', stacked, raw_echo.astype(jnp.float32), precision=PRECISION_MAX)
    return result.astype(jnp.bfloat16)

def focus(compressed, azimuth_phase):
    signal = lax.complex(compressed[:, 0].astype(jnp.float32), compressed[:, 1].astype(jnp.float32))
    spectrum = jnp.fft.fft(signal, axis=-1)
    doppler = lax.complex(jnp.cos(azimuth_phase), jnp.sin(azimuth_phase))
    image = jnp.fft.ifft(spectrum * doppler, axis=-1)
    return jnp.stack([jnp.real(image), jnp.imag(image)], axis=1).astype(jnp.bfloat16)

def interfere(focused, pair_offset):
    date_count = focused.shape[0]
    partner_index = (jnp.arange(date_count, dtype=jnp.int32) + pair_offset) % date_count
    current = focused.astype(jnp.float32)
    partner = jnp.take(current, partner_index, axis=0)
    real_part = current[:, 0] * partner[:, 0] + current[:, 1] * partner[:, 1]
    imag_part = current[:, 1] * partner[:, 0] - current[:, 0] * partner[:, 1]
    joined = jnp.stack([real_part, imag_part], axis=1)
    shape_all = joined.shape
    joined = joined.reshape(shape_all[0], 2, shape_all[2] // ML_RG, ML_RG, shape_all[3] // ML_AZ, ML_AZ)
    return lax.optimization_barrier(jnp.mean(joined, axis=(3, 5)))

def tri_window(patch_len):
    position = jnp.arange(patch_len, dtype=jnp.float32)
    return 1.0 - jnp.abs(position - (patch_len - 1) / 2.0) / (patch_len // 2)

def filter_patches(block_real, block_imag):
    spectra = jnp.fft.fft2(lax.complex(block_real, block_imag), axes=(2, 4))
    spectral = jnp.real(spectra) ** 2 + jnp.imag(spectra) ** 2
    smooth = jnp.zeros_like(spectral)
    for shift_gate in (-1, 0, 1):
        for shift_line in (-1, 0, 1):
            smooth = smooth + jnp.roll(spectral, (shift_gate, shift_line), axis=(2, 4))
    smooth = smooth / 9.0
    level_mean = lax.optimization_barrier(jnp.mean(smooth, axis=(2, 4), keepdims=True)) + 1e-06
    weight = jnp.sqrt(smooth / level_mean + BOX_FLOOR)
    inverse = jnp.fft.ifft2(spectra * weight, axes=(2, 4))
    window = tri_window(PATCH)
    window_two = window[:, None, None] * window[None, None, :]
    return (jnp.real(inverse) * window_two, jnp.imag(inverse) * window_two)

def goldstein(pad_real, pad_imag, gate_rows, line_cols):
    half_patch = PATCH // 2
    date_count = pad_real.shape[0]
    out_real = jnp.zeros((date_count, gate_rows, line_cols), jnp.float32)
    out_imag = jnp.zeros((date_count, gate_rows, line_cols), jnp.float32)
    for gate_odd in (0, 1):
        gate_start = gate_odd * half_patch
        gate_len = gate_rows + PATCH - 2 * gate_odd * half_patch
        gate_crop = half_patch - gate_start
        for line_odd in (0, 1):
            line_start = line_odd * half_patch
            line_len = line_cols + PATCH - 2 * line_odd * half_patch
            line_crop = half_patch - line_start
            shape_new = (date_count, gate_len // PATCH, PATCH, line_len // PATCH, PATCH)
            block_real = pad_real[:, gate_start:gate_start + gate_len, line_start:line_start + line_len].reshape(shape_new)
            block_imag = pad_imag[:, gate_start:gate_start + gate_len, line_start:line_start + line_len].reshape(shape_new)
            part_real, part_imag = filter_patches(block_real, block_imag)
            part_real = part_real.reshape(date_count, gate_len, line_len)
            part_imag = part_imag.reshape(date_count, gate_len, line_len)
            out_real = out_real + part_real[:, gate_crop:gate_crop + gate_rows, line_crop:line_crop + line_cols]
            out_imag = out_imag + part_imag[:, gate_crop:gate_crop + gate_rows, line_crop:line_crop + line_cols]
    return (out_real, out_imag)

def reference(raw_echo, range_filter, azimuth_phase, pair_offset):
    compressed = compress(raw_echo, range_filter)
    focused = focus(compressed, azimuth_phase)
    looks = interfere(focused, pair_offset)
    half_patch = PATCH // 2
    padded = jnp.pad(looks, ((0, 0), (0, 0), (half_patch, half_patch), (half_patch, half_patch)))
    out_real, out_imag = goldstein(padded[:, 0], padded[:, 1], looks.shape[2], looks.shape[3])
    return jnp.stack([out_real, out_imag], axis=1)
```

```python
import functools

import jax
import jax.numpy as jnp
import ml_dtypes
import numpy as np
from jax import lax
from jax.experimental import pallas as pl
from jax.experimental.pallas import tpu as pltpu
from jax.sharding import PartitionSpec as P

ML_RG = 4
ML_AZ = 2
PATCH = 32
HALF = PATCH // 2
BOX_FLOOR = 0.25
LANES = 128
VMEM = pl.BlockSpec(memory_space=pltpu.VMEM)


def right_block(table):
    return np.block([[table.real, table.imag], [-table.imag, table.real]])


def left_block(table):
    return np.block([[table.real, -table.imag], [table.imag, table.real]])


def split(value):
    high = value.astype(jnp.bfloat16)
    low = (value - high.astype(jnp.float32)).astype(jnp.bfloat16)
    return high, low


def mm(a, b):
    return jnp.dot(a, b, preferred_element_type=jnp.float32)


def exact_times(value, table):
    high, low = split(value)
    return mm(high, table) + mm(low, table)


def fft_leading(re, im, sign):
    count = len(re)
    if count == 1:
        return re, im
    if count == 2:
        return [re[0] + re[1], re[0] - re[1]], [im[0] + im[1], im[0] - im[1]]
    er, ei = fft_leading(re[0::2], im[0::2], sign)
    odr, odi = fft_leading(re[1::2], im[1::2], sign)
    half = count // 2
    out_r, out_i = [None] * count, [None] * count
    for k in range(half):
        angle = sign * 2.0 * np.pi * k / count
        c, s = float(np.cos(angle)), float(np.sin(angle))
        if k == 0:
            tr, ti = odr[k], odi[k]
        elif 4 * k == count:
            tr, ti = (-odi[k], odr[k]) if sign > 0 else (odi[k], -odr[k])
        else:
            tr = odr[k] * c - odi[k] * s
            ti = odr[k] * s + odi[k] * c
        out_r[k], out_i[k] = er[k] + tr, ei[k] + ti
        out_r[k + half], out_i[k + half] = er[k] - tr, ei[k] - ti
    return out_r, out_i


def filter_dates(
    cells_ref, rims_ref, enter_ref, extra_ref, gate_ref, near_gate_ref, near_line_ref, level_ref, gate_back_ref,
    line_back_ref, out_ref,
):
    dates, _, looks, gate_rows = out_ref.shape
    main = [cells_ref[date].astype(jnp.bfloat16) for date in range(dates)]
    rims = [rims_ref[pair].astype(jnp.bfloat16) for pair in range(dates // 2)]
    real, imag = [], []
    for date in range(dates):
        half = mm(jnp.concatenate([main[date], rims[date // 2]], axis=1), enter_ref[date % 2]).astype(jnp.bfloat16)
        width = half.shape[1] // 2
        real.append(half[:, :width])
        imag.append(half[:, width:])
    half = mm(jnp.concatenate(main + rims, axis=1), extra_ref[...]).astype(jnp.bfloat16)
    width = half.shape[1] // 2
    real.append(half[:, :width])
    imag.append(half[:, width:])
    image_re, image_im = [], []
    for first in range(0, dates + 1, 2):
        last = min(first + 2, dates + 1)
        re = jnp.concatenate(real[first:last], axis=1)
        im = jnp.concatenate(imag[first:last], axis=1)
        width = re.shape[1]
        spectra = mm(gate_ref[...], jnp.concatenate([re, im], axis=0))
        rows = spectra.shape[0] // 2
        re, im = spectra[:rows], spectra[rows:]
        power = re * re + im * im
        near = mm(near_gate_ref[...], power.astype(jnp.bfloat16))
        near = mm(near.astype(jnp.bfloat16), near_line_ref[:width, :width])
        sums = jnp.sum(power.reshape(rows // PATCH, PATCH, width), axis=1)
        level = exact_times(sums, level_ref[:width, :width])
        scale = 1.0 / (9.0 * (level + 1e-06))
        near = near.reshape(rows // PATCH, PATCH, width) * scale[:, None, :]
        weight = jnp.sqrt(near + BOX_FLOOR).reshape(rows, width)
        weighted = jnp.concatenate([re * weight, im * weight], axis=0).astype(jnp.bfloat16)
        image = mm(gate_back_ref[...], weighted).astype(jnp.bfloat16)
        step = width // (last - first)
        for start in range(0, width, step):
            image_re.append(image[:gate_rows, start : start + step])
            image_im.append(image[gate_rows:, start : start + step])
    contract = (((1,), (1,)), ((), ()))
    for date in range(dates):
        image = jnp.concatenate([image_re[date], image_im[date], image_re[dates], image_im[dates]], axis=1)
        result = lax.dot_general(line_back_ref[date], image, contract, preferred_element_type=jnp.float32)
        out_ref[date, 0] = result[:looks]
        out_ref[date, 1] = result[looks:]


def chunk_gates(gates):
    return gates // 2 if gates % (2 * 4 * ML_RG) == 0 else gates


def stack_kernel(
    shards, offset_ref, raw_hbm, filt_hbm, phase_hbm, *refs,
):
    count = (len(refs) - 17) // 2
    stored, out_ref, tables = refs[:count], refs[count], refs[count + 1 : 2 * count + 1]
    (raw_ref, filt_ref, phase_ref, sent, columns, turned, trig, work, focused, looks_sent, looks_got, cells, rims,
     send_sem, recv_sem, load_sem) = refs[2 * count + 1 :]
    twid_ref, fwd_ref, back_ref, gate_ref, main_ref, rim_ref = tables[:6]
    dates, _, line_count, total_gates = raw_ref.shape
    chunks, pairs, _, block_rows, lanes = columns.shape
    gates = total_gates // shards
    part_gates = gates // chunks
    me = lax.axis_index("lines")

    loads = [
        pltpu.make_async_copy(source, target, load_sem.at[i])
        for i, (source, target) in enumerate(
            [(filt_hbm, filt_ref), (raw_hbm, raw_ref), (phase_hbm, phase_ref)] + list(zip(stored, tables))
        )
    ]
    loads[0].start()
    loads[1].start()

    def ring(step):
        return lax.rem(me + step, shards)

    barrier = pltpu.get_barrier_semaphore()

    @pl.loop(1, shards)
    def _(step):
        pl.semaphore_signal(barrier, inc=1, device_id={"lines": ring(step)}, device_id_type=pl.DeviceIdType.MESH)

    for load in loads[2:]:
        load.start()

    def compress(chunk, pair):
        weights = filt_ref[...]
        if chunks > 1:
            weights = weights.reshape(2, shards, chunks, part_gates, total_gates)[:, :, chunk]
        weights = weights.reshape(2 * shards * part_gates, total_gates)
        half = shards * part_gates
        contract = (((1,), (1,)), ((), ()))
        for i in range(2):
            lines = raw_ref[2 * pair + i].reshape(2 * line_count, total_gates)
            product = lax.dot_general(weights, lines, contract, preferred_element_type=jnp.float32)
            real = product[:half, :line_count] - product[half:, line_count:]
            imag = product[half:, :line_count] + product[:half, line_count:]
            shape = (shards, part_gates, line_count)
            both = jnp.concatenate([real.reshape(shape), imag.reshape(shape)], axis=1)
            at = pl.ds(2 * i * part_gates, 2 * part_gates)
            sent[chunk, pair, :, at, :] = both.astype(jnp.bfloat16)

    def block(source, target, slot, peer):
        return pltpu.make_async_remote_copy(
            src_ref=source, dst_ref=target, send_sem=send_sem.at[slot], recv_sem=recv_sem.at[slot],
            device_id={"lines": peer}, device_id_type=pl.DeviceIdType.MESH,
        )

    def send_part(chunk, pair):
        slot = chunk * pairs + pair

        @pl.loop(1, shards)
        def _(step):
            peer = ring(step)
            block(sent.at[chunk, pair, peer], columns.at[chunk, pair, me], slot, peer).start()

        columns[chunk, pair, me] = sent[chunk, pair, me]

    def arrived(chunk, pair):
        part = pl.ds(0, shards - 1)
        slot = chunk * pairs + pair
        return block(sent.at[chunk, pair, part], columns.at[chunk, pair, part], slot, ring(1))

    def gathered(chunk):
        part = pl.ds(0, shards - 1)
        return block(looks_sent.at[chunk, part], looks_got.at[chunk, part], chunks * pairs + chunk, ring(1))

    loads[0].wait()
    loads[1].wait()
    for chunk in range(chunks):
        if chunk == 0:
            @pl.loop(0, pairs)
            def _(pair):
                compress(0, pair)

            pl.semaphore_wait(barrier, shards - 1)

            @pl.loop(0, pairs)
            def _(pair):
                send_part(0, pair)
        else:
            @pl.loop(0, pairs)
            def _(pair):
                compress(chunk, pair)
                send_part(chunk, pair)

    loads[2].wait()
    turned[...] = phase_ref[...].T

    @pl.loop(0, shards)
    def _(k):
        phase = turned[pl.ds(k, lanes, stride=shards), :].T
        at = pl.ds(pl.multiple_of(k * part_gates, part_gates), part_gates)
        cosine, sine = jnp.cos(phase), jnp.sin(phase)
        for chunk in range(chunks):
            trig[chunk, 0, at, :] = cosine[chunk * part_gates : (chunk + 1) * part_gates]
            trig[chunk, 1, at, :] = sine[chunk * part_gates : (chunk + 1) * part_gates]

    for load in loads[3:9]:
        load.wait()
    rows = shards * part_gates
    looks_rows = gate_ref.shape[0] // 3
    tile = looks_rows // shards

    @pl.loop(0, chunks)
    def _(chunk):
        @pl.loop(0, pairs)
        def _(pair):
            arrived(chunk, pair).wait_recv()
            for i in range(2):
                start = 2 * i * part_gates
                data = [
                    columns[chunk, pair, s, pl.ds(start, 2 * part_gates), :].astype(jnp.float32) for s in range(shards)
                ]
                for low in range(0, part_gates, 8):
                    re = [value[low : low + 8] for value in data]
                    im = [value[part_gates + low : part_gates + low + 8] for value in data]
                    re, im = fft_leading(re, im, -1.0)
                    for k in range(shards):
                        c, s = twid_ref[0, pl.ds(k, 1), :], twid_ref[1, pl.ds(k, 1), :]
                        at = pl.ds(i * rows + k * part_gates + low, 8)
                        work[at, :lanes] = re[k] * c + im[k] * s
                        work[at, lanes:] = im[k] * c - re[k] * s
            spectrum = mm(work[...].astype(jnp.bfloat16), fwd_ref[...])
            c, s = trig[chunk, 0], trig[chunk, 1]
            shifted = []
            for i in range(2):
                re, im = spectrum[i * rows : (i + 1) * rows, :lanes], spectrum[i * rows : (i + 1) * rows, lanes:]
                shifted.append(jnp.concatenate([re * c - im * s, re * s + im * c], axis=1))
            work[...] = mm(jnp.concatenate(shifted, axis=0).astype(jnp.bfloat16), back_ref[...])
            for i in range(2):
                for low in range(0, part_gates, 8):
                    re, im = [], []
                    for k in range(shards):
                        c, s = twid_ref[0, pl.ds(k, 1), :], twid_ref[1, pl.ds(k, 1), :]
                        at = pl.ds(i * rows + k * part_gates + low, 8)
                        a, b = work[at, :lanes], work[at, lanes:]
                        re.append(a * c - b * s)
                        im.append(b * c + a * s)
                    re, im = fft_leading(re, im, 1.0)
                    for n in range(shards):
                        at = pl.ds(n * part_gates + low, 8)
                        focused[2 * pair + i, at, :lanes] = re[n].astype(jnp.bfloat16).astype(jnp.float32)
                        focused[2 * pair + i, at, lanes:] = im[n].astype(jnp.bfloat16).astype(jnp.float32)

        pieces, rim = [], None
        for parity in range(2):
            joined = []
            for d in (parity, parity + 2):
                partner = lax.rem(d + offset_ref[d], dates)
                a, b = focused[d, :, :lanes], focused[d, :, lanes:]
                p, q = focused[partner, :, :lanes], focused[partner, :, lanes:]
                joined.append(jnp.concatenate([a * p + b * q, b * p - a * q], axis=1).astype(jnp.bfloat16))
            summed = mm(gate_ref[...], jnp.concatenate(joined, axis=0)).astype(jnp.bfloat16)
            pieces.append(mm(summed[:looks_rows], main_ref[...]))
            sides = jnp.concatenate([summed[looks_rows : 2 * looks_rows], summed[2 * looks_rows :]], axis=1)
            side = mm(sides, rim_ref[parity])
            rim = side if rim is None else rim + side
        shaped = [piece.reshape(shards, tile, lanes) for piece in pieces + [rim]]
        looks_sent[chunk] = jnp.concatenate(shaped, axis=1).astype(looks_sent.dtype)

        @pl.loop(1, shards)
        def _(step):
            peer = ring(step)
            block(looks_sent.at[chunk, peer], looks_got.at[chunk, me], chunks * pairs + chunk, peer).start()

        looks_got[chunk, me] = looks_sent[chunk, me]

    for load in loads[9:]:
        load.wait()

    @pl.loop(0, chunks)
    def _(chunk):
        @pl.loop(0, pairs)
        def _(pair):
            arrived(chunk, pair).wait_send()

    part_looks = tile // 2
    for chunk in range(chunks):
        gathered(chunk).wait_recv()
        for shard in range(shards):
            received = looks_got[chunk, shard].astype(jnp.float32)
            at = pl.ds((shard * chunks + chunk) * part_looks, part_looks)
            for q in range(2):
                for parity in range(2):
                    low = parity * tile + q * part_looks
                    cells[2 * q + parity, at, :] = received[low : low + part_looks]
                low = 2 * tile + q * part_looks
                rims[q, at, :] = received[low : low + part_looks]

    filter_dates(cells, rims, *tables[6:], out_ref)

    @pl.loop(0, chunks)
    def _(chunk):
        gathered(chunk).wait_send()


def focus_tables(shards, part_gates, lanes):
    total = shards * lanes
    k1, n2 = np.arange(shards), np.arange(lanes)
    angle = 2.0 * np.pi / total * (np.outer(k1, n2) % total)
    twiddle = np.stack([np.cos(angle), np.sin(angle)]).astype(np.float32)
    grid = np.exp(-2j * np.pi / lanes * (np.outer(n2, n2) % lanes))
    forward = right_block(grid)
    backward = right_block(np.conj(grid)) / total
    group = np.kron(np.eye(part_gates // ML_RG), np.ones((1, ML_RG)))
    gate_sum = []
    for shift in (0, -1, 1):
        spread = np.einsum("js,qr,lg->jqlrsg", np.eye(shards, k=shift), np.eye(2), group)
        gate_sum.append(spread.reshape(shards * 2 * group.shape[0], -1))
    gate_sum = np.concatenate(gate_sum)
    looks = lanes // ML_AZ
    pair = np.kron(np.eye(looks), np.ones((ML_AZ, 1))) / (ML_RG * ML_AZ)
    main = np.kron(np.eye(2), pair)
    rim = np.zeros((2, 4 * lanes, lanes))
    for parity in range(2):
        for part in range(2):
            low = parity * 4 * HALF + part * 2 * HALF
            source = part * lanes
            rim[parity, source : source + lanes, low : low + HALF] = pair[:, looks - HALF :]
            source += 2 * lanes
            rim[parity, source : source + lanes, low + HALF : low + 2 * HALF] = pair[:, :HALF]
    bf16 = ml_dtypes.bfloat16
    return twiddle, forward.astype(bf16), backward.astype(bf16), gate_sum.astype(bf16), main.astype(bf16), rim.astype(bf16)


def filtered_looks(raw_echo, range_filter, azimuth_phase, pair_offset, shards):
    dates, _, lanes, total_gates = raw_echo.shape
    gates = azimuth_phase.shape[0]
    part_gates = chunk_gates(gates)
    chunks, pairs = gates // part_gates, dates // 2
    gate_rows, looks = total_gates // ML_RG, lanes // ML_AZ
    tables = focus_tables(shards, part_gates, lanes) + filter_tables(gate_rows, looks, dates)
    rows = shards * part_gates
    block = (chunks, shards, 6 * (part_gates // ML_RG), lanes)
    columns = (chunks, pairs, shards, 4 * part_gates, lanes)
    return pl.pallas_call(
        functools.partial(stack_kernel, shards),
        in_specs=[pl.BlockSpec(memory_space=pltpu.SMEM)]
        + [pl.BlockSpec(memory_space=pl.ANY)] * (3 + len(tables)),
        out_specs=VMEM,
        out_shape=jax.ShapeDtypeStruct((dates, 2, looks, gate_rows), jnp.float32),
        scratch_shapes=[pltpu.VMEM(table.shape, table.dtype) for table in tables]
        + [
            pltpu.VMEM(raw_echo.shape, raw_echo.dtype),
            pltpu.VMEM(range_filter.shape, range_filter.dtype),
            pltpu.VMEM(azimuth_phase.shape, azimuth_phase.dtype),
            pltpu.VMEM(columns, jnp.bfloat16),
            pltpu.VMEM(columns, jnp.bfloat16),
            pltpu.VMEM(azimuth_phase.shape[::-1], jnp.float32),
            pltpu.VMEM((chunks, 2, rows, lanes), jnp.float32),
            pltpu.VMEM((2 * rows, 2 * lanes), jnp.float32),
            pltpu.VMEM((dates, rows, 2 * lanes), jnp.float32),
            pltpu.VMEM(block, jnp.bfloat16),
            pltpu.VMEM(block, jnp.bfloat16),
            pltpu.VMEM((dates, gate_rows, 2 * looks), jnp.float32),
            pltpu.VMEM((pairs, gate_rows, 2 * looks), jnp.float32),
            pltpu.SemaphoreType.DMA((chunks * (pairs + 1),)),
            pltpu.SemaphoreType.DMA((chunks * (pairs + 1),)),
            pltpu.SemaphoreType.DMA((3 + len(tables),)),
        ],
        compiler_params=pltpu.CompilerParams(collective_id=0, has_side_effects=True),
        name="stack",
    )(pair_offset, raw_echo, range_filter, azimuth_phase, *tables)


def tri_window():
    return 1.0 - np.abs(np.arange(PATCH) - (PATCH - 1) / 2.0) / HALF


def patch_maps(cells, starts):
    count = len(starts)
    forward = np.zeros((cells, count, PATCH), np.complex128)
    backward = np.zeros((count, PATCH, cells), np.complex128)
    window, k = tri_window(), np.arange(PATCH)
    for patch, start in enumerate(starts):
        for a in range(PATCH):
            cell = start + a
            if 0 <= cell < cells:
                wave = np.exp(2j * np.pi / PATCH * (k * a % PATCH))
                forward[cell, patch] = np.conj(wave)
                backward[patch, :, cell] = wave * window[a] / PATCH
    return forward.reshape(cells, -1), backward.reshape(-1, cells)


def filter_tables(gate_rows, looks, dates):
    gate_starts = range(-HALF, gate_rows - HALF + 1, HALF)
    line_starts = range(0, looks + 1, HALF)
    gate_fwd, gate_back = patch_maps(gate_rows, gate_starts)
    line_fwd, _ = patch_maps(looks + PATCH, line_starts)
    _, line_back = patch_maps(looks, [start - HALF for start in line_starts])
    width = (len(line_starts) - 1) * PATCH
    span = 2 * looks

    def entry(columns, main, low, table):
        block = right_block(columns).reshape(2, looks + PATCH, -1)
        for part in range(2):
            table[main + part * looks : main + (part + 1) * looks] += block[part, HALF : HALF + looks]
            at = low + part * 2 * HALF
            table[at : at + HALF] += block[part, :HALF]
            table[at + HALF : at + 2 * HALF] += block[part, HALF + looks :]

    enter = np.zeros((2, 2 * span, 2 * width))
    for parity in range(2):
        entry(line_fwd[:, :width], 0, span + parity * 4 * HALF, enter[parity])
    wide = dates * PATCH
    extra = np.zeros((dates * span + dates // 2 * span, 2 * wide))
    back = np.zeros((dates, 2 * looks, 2 * width + 2 * wide))
    for date in range(dates):
        placed = np.zeros((looks + PATCH, wide), np.complex128)
        placed[:, date * PATCH : (date + 1) * PATCH] = line_fwd[:, width:]
        entry(placed, date * span, dates * span + date // 2 * span + date % 2 * 4 * HALF, extra)
        placed = np.zeros((wide, looks), np.complex128)
        placed[date * PATCH : (date + 1) * PATCH] = line_back[width:]
        back[date, :, : 2 * width] = right_block(line_back[:width]).T
        back[date, :, 2 * width :] = right_block(placed).T
    gap = (np.arange(PATCH)[:, None] - np.arange(PATCH)[None, :]) % PATCH
    near = (gap <= 1) | (gap == PATCH - 1)
    group = max(2 * width, wide) // PATCH
    bf16 = ml_dtypes.bfloat16
    near_gate = np.kron(np.eye(len(gate_starts)), near).astype(bf16)
    near_line = np.kron(np.eye(group), near).astype(bf16)
    level = np.kron(np.eye(group), np.ones((PATCH, PATCH)) / PATCH**2).astype(bf16)
    return (
        enter.astype(bf16),
        extra.astype(bf16),
        left_block(gate_fwd.T).astype(bf16),
        near_gate,
        near_line,
        level,
        left_block(gate_back.T).astype(bf16),
        back.astype(bf16),
    )


def body(raw_echo, range_filter, azimuth_phase, pair_offset):
    shards = lax.axis_size("lines")
    image = filtered_looks(raw_echo, range_filter, azimuth_phase, pair_offset, shards)
    return image.transpose(0, 1, 3, 2)


def solution(mesh):
    placed = (P("groups", None, "lines", None), P(), P("lines", None), P())
    return jax.shard_map(
        body,
        mesh=mesh,
        in_specs=placed,
        out_specs=P("groups", None, None, "lines"),
        check_vma=False,
    )
```

```python
import functools

import jax
import jax.numpy as jnp
import ml_dtypes
import numpy as np
from jax import lax
from jax.experimental import pallas as pl
from jax.experimental.pallas import tpu as pltpu
from jax.sharding import PartitionSpec as P

ML_RG = 4
ML_AZ = 2
PATCH = 32
HALF = PATCH // 2
BOX_FLOOR = 0.25
LANES = 128
VMEM = pl.BlockSpec(memory_space=pltpu.VMEM)


def right_block(table):
    return np.block([[table.real, table.imag], [-table.imag, table.real]])


def left_block(table):
    return np.block([[table.real, -table.imag], [table.imag, table.real]])


def split(value):
    high = value.astype(jnp.bfloat16)
    low = (value - high.astype(jnp.float32)).astype(jnp.bfloat16)
    return high, low


def mm(a, b):
    return jnp.dot(a, b, preferred_element_type=jnp.float32)


def exact_times(value, table):
    high, low = split(value)
    return mm(high, table) + mm(low, table)


def fft_leading(re, im, sign):
    count = len(re)
    if count == 1:
        return re, im
    if count == 2:
        return [re[0] + re[1], re[0] - re[1]], [im[0] + im[1], im[0] - im[1]]
    er, ei = fft_leading(re[0::2], im[0::2], sign)
    odr, odi = fft_leading(re[1::2], im[1::2], sign)
    half = count // 2
    out_r, out_i = [None] * count, [None] * count
    for k in range(half):
        angle = sign * 2.0 * np.pi * k / count
        c, s = float(np.cos(angle)), float(np.sin(angle))
        if k == 0:
            tr, ti = odr[k], odi[k]
        elif 4 * k == count:
            tr, ti = (-odi[k], odr[k]) if sign > 0 else (odi[k], -odr[k])
        else:
            tr = odr[k] * c - odi[k] * s
            ti = odr[k] * s + odi[k] * c
        out_r[k], out_i[k] = er[k] + tr, ei[k] + ti
        out_r[k + half], out_i[k + half] = er[k] - tr, ei[k] - ti
    return out_r, out_i


def filter_dates(
    cells_ref, rims_ref, table, out_ref,
):
    dates, _, looks, gate_rows = out_ref.shape
    main = [cells_ref[date].astype(jnp.bfloat16) for date in range(dates)]
    rims = [rims_ref[pair].astype(jnp.bfloat16) for pair in range(dates // 2)]
    real, imag = [], []
    for date in range(dates):
        half = mm(jnp.concatenate([main[date], rims[date // 2]], axis=1), table("enter", date % 2)).astype(jnp.bfloat16)
        width = half.shape[1] // 2
        real.append(half[:, :width])
        imag.append(half[:, width:])
    half = mm(jnp.concatenate(main + rims, axis=1), table("extra")).astype(jnp.bfloat16)
    width = half.shape[1] // 2
    real.append(half[:, :width])
    imag.append(half[:, width:])
    image_re, image_im = [], []
    for first in range(0, dates + 1, 2):
        last = min(first + 2, dates + 1)
        re = jnp.concatenate(real[first:last], axis=1)
        im = jnp.concatenate(imag[first:last], axis=1)
        width = re.shape[1]
        spectra = mm(table("gate_fwd"), jnp.concatenate([re, im], axis=0))
        rows = spectra.shape[0] // 2
        re, im = spectra[:rows], spectra[rows:]
        power = re * re + im * im
        near = mm(table("near_gate"), power.astype(jnp.bfloat16))
        near = mm(near.astype(jnp.bfloat16), table("near_line")[:width, :width])
        sums = jnp.sum(power.reshape(rows // PATCH, PATCH, width), axis=1)
        level = exact_times(sums, table("level")[:width, :width])
        scale = 1.0 / (9.0 * (level + 1e-06))
        near = near.reshape(rows // PATCH, PATCH, width) * scale[:, None, :]
        weight = jnp.sqrt(near + BOX_FLOOR).reshape(rows, width)
        weighted = jnp.concatenate([re * weight, im * weight], axis=0).astype(jnp.bfloat16)
        image = mm(table("gate_back"), weighted).astype(jnp.bfloat16)
        step = width // (last - first)
        for start in range(0, width, step):
            image_re.append(image[:gate_rows, start : start + step])
            image_im.append(image[gate_rows:, start : start + step])
    contract = (((1,), (1,)), ((), ()))
    for date in range(dates):
        image = jnp.concatenate([image_re[date], image_im[date], image_re[dates], image_im[dates]], axis=1)
        result = lax.dot_general(table("line_back", date), image, contract, preferred_element_type=jnp.float32)
        out_ref[date, 0] = result[:looks]
        out_ref[date, 1] = result[looks:]


def chunk_gates(gates):
    return gates // 2 if gates % (2 * 4 * ML_RG) == 0 else gates


def stack_kernel(
    shards, places, offset_hbm, raw_hbm, filt_hbm, phase_hbm, pack_hbm, out_ref, pack, raw_ref, filt_ref, phase_ref,
    sent, columns, turned, trig, twid_ref, work, focused, looks_sent, looks_got, cells, rims, offset_ref, send_sem, recv_sem, load_sem,
):
    def table(name, index=0):
        first, height, panels, width = places[name]
        first += index * height * panels
        parts = [pack[first + i * height : first + (i + 1) * height, :] for i in range(panels)]
        whole = parts[0] if panels == 1 else jnp.concatenate(parts, axis=1)
        return whole[:, :width]

    dates, _, line_count, total_gates = raw_ref.shape
    chunks, pairs, _, block_rows, lanes = columns.shape
    gates = total_gates // shards
    part_gates = gates // chunks
    me = lax.axis_index("lines")

    loads = [
        pltpu.make_async_copy(source, target, load_sem.at[i])
        for i, (source, target) in enumerate(
            [(filt_hbm, filt_ref), (raw_hbm, raw_ref), (phase_hbm, phase_ref), (pack_hbm, pack), (offset_hbm, offset_ref)]
        )
    ]
    loads[0].start()
    loads[1].start()

    def ring(step):
        return lax.rem(me + step, shards)

    barrier = pltpu.get_barrier_semaphore()

    @pl.loop(1, shards)
    def _(step):
        pl.semaphore_signal(barrier, inc=1, device_id={"lines": ring(step)}, device_id_type=pl.DeviceIdType.MESH)

    for load in loads[2:]:
        load.start()

    def compress(chunk, pair):
        weights = filt_ref[...]
        if chunks > 1:
            weights = weights.reshape(2, shards, chunks, part_gates, total_gates)[:, :, chunk]
        weights = weights.reshape(2 * shards * part_gates, total_gates)
        half = shards * part_gates
        contract = (((1,), (1,)), ((), ()))
        for i in range(2):
            lines = raw_ref[2 * pair + i].reshape(2 * line_count, total_gates)
            product = lax.dot_general(weights, lines, contract, preferred_element_type=jnp.float32)
            real = product[:half, :line_count] - product[half:, line_count:]
            imag = product[half:, :line_count] + product[:half, line_count:]
            shape = (shards, part_gates, line_count)
            both = jnp.concatenate([real.reshape(shape), imag.reshape(shape)], axis=1)
            at = pl.ds(2 * i * part_gates, 2 * part_gates)
            sent[chunk, pair, :, at, :] = both.astype(jnp.bfloat16)

    def block(source, target, slot, peer):
        return pltpu.make_async_remote_copy(
            src_ref=source, dst_ref=target, send_sem=send_sem.at[slot], recv_sem=recv_sem.at[slot],
            device_id={"lines": peer}, device_id_type=pl.DeviceIdType.MESH,
        )

    def send_part(chunk, pair):
        slot = chunk * pairs + pair

        @pl.loop(1, shards)
        def _(step):
            peer = ring(step)
            block(sent.at[chunk, pair, peer], columns.at[chunk, pair, me], slot, peer).start()

        columns[chunk, pair, me] = sent[chunk, pair, me]

    def arrived(chunk, pair):
        part = pl.ds(0, shards - 1)
        slot = chunk * pairs + pair
        return block(sent.at[chunk, pair, part], columns.at[chunk, pair, part], slot, ring(1))

    def gathered(chunk):
        part = pl.ds(0, shards - 1)
        return block(looks_sent.at[chunk, part], looks_got.at[chunk, part], chunks * pairs + chunk, ring(1))

    loads[0].wait()
    loads[1].wait()
    for chunk in range(chunks):
        if chunk == 0:
            @pl.loop(0, pairs)
            def _(pair):
                compress(0, pair)

            pl.semaphore_wait(barrier, shards - 1)

            @pl.loop(0, pairs)
            def _(pair):
                send_part(0, pair)
        else:
            @pl.loop(0, pairs)
            def _(pair):
                compress(chunk, pair)
                send_part(chunk, pair)

    loads[2].wait()
    turned[...] = phase_ref[...].T

    @pl.loop(0, shards)
    def _(k):
        phase = turned[pl.ds(k, lanes, stride=shards), :].T
        at = pl.ds(pl.multiple_of(k * part_gates, part_gates), part_gates)
        cosine, sine = jnp.cos(phase), jnp.sin(phase)
        for chunk in range(chunks):
            trig[chunk, 0, at, :] = cosine[chunk * part_gates : (chunk + 1) * part_gates]
            trig[chunk, 1, at, :] = sine[chunk * part_gates : (chunk + 1) * part_gates]

    loads[3].wait()
    loads[4].wait()
    pieces = table("twiddle").astype(jnp.float32)
    count = twid_ref.shape[0]
    twid_ref[...] = pieces[:count] + pieces[count : 2 * count] + pieces[2 * count :]
    rows = shards * part_gates
    looks_rows = places["gate_sum"][1] // 3
    tile = looks_rows // shards

    @pl.loop(0, chunks)
    def _(chunk):
        @pl.loop(0, pairs)
        def _(pair):
            arrived(chunk, pair).wait_recv()
            for i in range(2):
                start = 2 * i * part_gates
                data = [
                    columns[chunk, pair, s, pl.ds(start, 2 * part_gates), :].astype(jnp.float32) for s in range(shards)
                ]
                for low in range(0, part_gates, 8):
                    re = [value[low : low + 8] for value in data]
                    im = [value[part_gates + low : part_gates + low + 8] for value in data]
                    re, im = fft_leading(re, im, -1.0)
                    for k in range(shards):
                        c, s = twid_ref[pl.ds(k, 1), :], twid_ref[pl.ds(shards + k, 1), :]
                        at = pl.ds(i * rows + k * part_gates + low, 8)
                        work[at, :lanes] = re[k] * c + im[k] * s
                        work[at, lanes:] = im[k] * c - re[k] * s
            spectrum = mm(work[...].astype(jnp.bfloat16), table("forward"))
            c, s = trig[chunk, 0], trig[chunk, 1]
            shifted = []
            for i in range(2):
                re, im = spectrum[i * rows : (i + 1) * rows, :lanes], spectrum[i * rows : (i + 1) * rows, lanes:]
                shifted.append(jnp.concatenate([re * c - im * s, re * s + im * c], axis=1))
            work[...] = mm(jnp.concatenate(shifted, axis=0).astype(jnp.bfloat16), table("backward"))
            for i in range(2):
                for low in range(0, part_gates, 8):
                    re, im = [], []
                    for k in range(shards):
                        c, s = twid_ref[pl.ds(k, 1), :], twid_ref[pl.ds(shards + k, 1), :]
                        at = pl.ds(i * rows + k * part_gates + low, 8)
                        a, b = work[at, :lanes], work[at, lanes:]
                        re.append(a * c - b * s)
                        im.append(b * c + a * s)
                    re, im = fft_leading(re, im, 1.0)
                    for n in range(shards):
                        at = pl.ds(n * part_gates + low, 8)
                        focused[2 * pair + i, at, :lanes] = re[n].astype(jnp.bfloat16).astype(jnp.float32)
                        focused[2 * pair + i, at, lanes:] = im[n].astype(jnp.bfloat16).astype(jnp.float32)

        pieces, rim = [], None
        for parity in range(2):
            joined = []
            for d in (parity, parity + 2):
                partner = lax.rem(d + offset_ref[d], dates)
                a, b = focused[d, :, :lanes], focused[d, :, lanes:]
                p, q = focused[partner, :, :lanes], focused[partner, :, lanes:]
                joined.append(jnp.concatenate([a * p + b * q, b * p - a * q], axis=1).astype(jnp.bfloat16))
            summed = mm(table("gate_sum"), jnp.concatenate(joined, axis=0)).astype(jnp.bfloat16)
            pieces.append(mm(summed[:looks_rows], table("main")))
            sides = jnp.concatenate([summed[looks_rows : 2 * looks_rows], summed[2 * looks_rows :]], axis=1)
            side = mm(sides, table("rim", parity))
            rim = side if rim is None else rim + side
        shaped = [piece.reshape(shards, tile, lanes) for piece in pieces + [rim]]
        looks_sent[chunk] = jnp.concatenate(shaped, axis=1).astype(looks_sent.dtype)

        @pl.loop(1, shards)
        def _(step):
            peer = ring(step)
            block(looks_sent.at[chunk, peer], looks_got.at[chunk, me], chunks * pairs + chunk, peer).start()

        looks_got[chunk, me] = looks_sent[chunk, me]

    @pl.loop(0, chunks)
    def _(chunk):
        @pl.loop(0, pairs)
        def _(pair):
            arrived(chunk, pair).wait_send()

    part_looks = tile // 2
    for chunk in range(chunks):
        gathered(chunk).wait_recv()
        for shard in range(shards):
            received = looks_got[chunk, shard].astype(jnp.float32)
            at = pl.ds((shard * chunks + chunk) * part_looks, part_looks)
            for q in range(2):
                for parity in range(2):
                    low = parity * tile + q * part_looks
                    cells[2 * q + parity, at, :] = received[low : low + part_looks]
                low = 2 * tile + q * part_looks
                rims[q, at, :] = received[low : low + part_looks]

    filter_dates(cells, rims, table, out_ref)

    @pl.loop(0, chunks)
    def _(chunk):
        gathered(chunk).wait_send()


def focus_tables(shards, part_gates, lanes):
    total = shards * lanes
    k1, n2 = np.arange(shards), np.arange(lanes)
    angle = 2.0 * np.pi / total * (np.outer(k1, n2) % total)
    twiddle = np.stack([np.cos(angle), np.sin(angle)]).astype(np.float32)
    grid = np.exp(-2j * np.pi / lanes * (np.outer(n2, n2) % lanes))
    forward = right_block(grid)
    backward = right_block(np.conj(grid)) / total
    group = np.kron(np.eye(part_gates // ML_RG), np.ones((1, ML_RG)))
    gate_sum = []
    for shift in (0, -1, 1):
        spread = np.einsum("js,qr,lg->jqlrsg", np.eye(shards, k=shift), np.eye(2), group)
        gate_sum.append(spread.reshape(shards * 2 * group.shape[0], -1))
    gate_sum = np.concatenate(gate_sum)
    looks = lanes // ML_AZ
    pair = np.kron(np.eye(looks), np.ones((ML_AZ, 1))) / (ML_RG * ML_AZ)
    main = np.kron(np.eye(2), pair)
    rim = np.zeros((2, 4 * lanes, lanes))
    for parity in range(2):
        for part in range(2):
            low = parity * 4 * HALF + part * 2 * HALF
            source = part * lanes
            rim[parity, source : source + lanes, low : low + HALF] = pair[:, looks - HALF :]
            source += 2 * lanes
            rim[parity, source : source + lanes, low + HALF : low + 2 * HALF] = pair[:, :HALF]
    twiddle = twiddle.reshape(2 * shards, lanes)
    high = twiddle.astype(ml_dtypes.bfloat16).astype(np.float32)
    middle = (twiddle - high).astype(ml_dtypes.bfloat16).astype(np.float32)
    pieces = np.concatenate([high, middle, twiddle - high - middle])
    return {
        "twiddle": pieces, "forward": forward, "backward": backward, "gate_sum": gate_sum, "main": main, "rim": rim,
    }


def filtered_looks(raw_echo, range_filter, azimuth_phase, pair_offset, shards):
    dates, _, lanes, total_gates = raw_echo.shape
    gates = azimuth_phase.shape[0]
    part_gates = chunk_gates(gates)
    chunks, pairs = gates // part_gates, dates // 2
    gate_rows, looks = total_gates // ML_RG, lanes // ML_AZ
    tables = focus_tables(shards, part_gates, lanes)
    tables.update(filter_tables(gate_rows, looks, dates))
    places, pack = packed(tables)
    rows = shards * part_gates
    block = (chunks, shards, 6 * (part_gates // ML_RG), lanes)
    columns = (chunks, pairs, shards, 4 * part_gates, lanes)
    return pl.pallas_call(
        functools.partial(stack_kernel, shards, places),
        in_specs=[pl.BlockSpec(memory_space=pl.ANY)] * 5,
        out_specs=VMEM,
        out_shape=jax.ShapeDtypeStruct((dates, 2, looks, gate_rows), jnp.float32),
        scratch_shapes=[
            pltpu.VMEM(pack.shape, pack.dtype),
            pltpu.VMEM(raw_echo.shape, raw_echo.dtype),
            pltpu.VMEM(range_filter.shape, range_filter.dtype),
            pltpu.VMEM(azimuth_phase.shape, azimuth_phase.dtype),
            pltpu.VMEM(columns, jnp.bfloat16),
            pltpu.VMEM(columns, jnp.bfloat16),
            pltpu.VMEM(azimuth_phase.shape[::-1], jnp.float32),
            pltpu.VMEM((chunks, 2, rows, lanes), jnp.float32),
            pltpu.VMEM((2 * shards, lanes), jnp.float32),
            pltpu.VMEM((2 * rows, 2 * lanes), jnp.float32),
            pltpu.VMEM((dates, rows, 2 * lanes), jnp.float32),
            pltpu.VMEM(block, jnp.bfloat16),
            pltpu.VMEM(block, jnp.bfloat16),
            pltpu.VMEM((dates, gate_rows, 2 * looks), jnp.float32),
            pltpu.VMEM((pairs, gate_rows, 2 * looks), jnp.float32),
            pltpu.SMEM(pair_offset.shape, pair_offset.dtype),
            pltpu.SemaphoreType.DMA((chunks * (pairs + 1),)),
            pltpu.SemaphoreType.DMA((chunks * (pairs + 1),)),
            pltpu.SemaphoreType.DMA((5,)),
        ],
        compiler_params=pltpu.CompilerParams(collective_id=0, has_side_effects=True, vmem_limit_bytes=54784 * 1024),
        name="stack",
    )(pair_offset, raw_echo, range_filter, azimuth_phase, pack)


def tri_window():
    return 1.0 - np.abs(np.arange(PATCH) - (PATCH - 1) / 2.0) / HALF


def patch_maps(cells, starts):
    count = len(starts)
    forward = np.zeros((cells, count, PATCH), np.complex128)
    backward = np.zeros((count, PATCH, cells), np.complex128)
    window, k = tri_window(), np.arange(PATCH)
    for patch, start in enumerate(starts):
        for a in range(PATCH):
            cell = start + a
            if 0 <= cell < cells:
                wave = np.exp(2j * np.pi / PATCH * (k * a % PATCH))
                forward[cell, patch] = np.conj(wave)
                backward[patch, :, cell] = wave * window[a] / PATCH
    return forward.reshape(cells, -1), backward.reshape(-1, cells)


def filter_tables(gate_rows, looks, dates):
    gate_starts = range(-HALF, gate_rows - HALF + 1, HALF)
    line_starts = range(0, looks + 1, HALF)
    gate_fwd, gate_back = patch_maps(gate_rows, gate_starts)
    line_fwd, _ = patch_maps(looks + PATCH, line_starts)
    _, line_back = patch_maps(looks, [start - HALF for start in line_starts])
    width = (len(line_starts) - 1) * PATCH
    span = 2 * looks

    def entry(columns, main, low, table):
        block = right_block(columns).reshape(2, looks + PATCH, -1)
        for part in range(2):
            table[main + part * looks : main + (part + 1) * looks] += block[part, HALF : HALF + looks]
            at = low + part * 2 * HALF
            table[at : at + HALF] += block[part, :HALF]
            table[at + HALF : at + 2 * HALF] += block[part, HALF + looks :]

    enter = np.zeros((2, 2 * span, 2 * width))
    for parity in range(2):
        entry(line_fwd[:, :width], 0, span + parity * 4 * HALF, enter[parity])
    wide = dates * PATCH
    extra = np.zeros((dates * span + dates // 2 * span, 2 * wide))
    back = np.zeros((dates, 2 * looks, 2 * width + 2 * wide))
    for date in range(dates):
        placed = np.zeros((looks + PATCH, wide), np.complex128)
        placed[:, date * PATCH : (date + 1) * PATCH] = line_fwd[:, width:]
        entry(placed, date * span, dates * span + date // 2 * span + date % 2 * 4 * HALF, extra)
        placed = np.zeros((wide, looks), np.complex128)
        placed[date * PATCH : (date + 1) * PATCH] = line_back[width:]
        back[date, :, : 2 * width] = right_block(line_back[:width]).T
        back[date, :, 2 * width :] = right_block(placed).T
    gap = (np.arange(PATCH)[:, None] - np.arange(PATCH)[None, :]) % PATCH
    near = (gap <= 1) | (gap == PATCH - 1)
    group = max(2 * width, wide) // PATCH
    near_gate = np.kron(np.eye(len(gate_starts)), near)
    near_line = np.kron(np.eye(group), near)
    level = np.kron(np.eye(group), np.ones((PATCH, PATCH)) / PATCH**2)
    return {
        "enter": enter,
        "extra": extra,
        "gate_fwd": left_block(gate_fwd.T),
        "near_gate": near_gate,
        "near_line": near_line,
        "level": level,
        "gate_back": left_block(gate_back.T),
        "line_back": back,
    }


def packed(tables):
    places, panels, first = {}, [], 0
    for name, table in tables.items():
        stack = table.reshape((-1,) + table.shape[-2:])
        _, height, width = stack.shape
        count = -(-width // LANES)
        places[name] = (first, height, count, width)
        for part in np.pad(stack, ((0, 0), (0, 0), (0, count * LANES - width))):
            for i in range(count):
                panels.append(part[:, i * LANES : (i + 1) * LANES])
                first += height
    return places, np.concatenate(panels).astype(ml_dtypes.bfloat16)


def body(raw_echo, range_filter, azimuth_phase, pair_offset):
    shards = lax.axis_size("lines")
    image = filtered_looks(raw_echo, range_filter, azimuth_phase, pair_offset, shards)
    return image.transpose(0, 1, 3, 2)


def solution(mesh):
    placed = (P("groups", None, "lines", None), P(), P("lines", None), P())
    return jax.shard_map(
        body,
        mesh=mesh,
        in_specs=placed,
        out_specs=P("groups", None, None, "lines"),
        check_vma=False,
    )
```

```python
import functools

import jax
import jax.numpy as jnp
import ml_dtypes
import numpy as np
from jax import lax
from jax.experimental import pallas as pl
from jax.experimental.pallas import tpu as pltpu
from jax.sharding import PartitionSpec as P

ML_RG = 4
ML_AZ = 2
PATCH = 32
HALF = PATCH // 2
BOX_FLOOR = 0.25
LANES = 128
VMEM = pl.BlockSpec(memory_space=pltpu.VMEM)


def right_block(table):
    return np.block([[table.real, table.imag], [-table.imag, table.real]])


def left_block(table):
    return np.block([[table.real, -table.imag], [table.imag, table.real]])


def split(value):
    high = value.astype(jnp.bfloat16)
    low = (value - high.astype(jnp.float32)).astype(jnp.bfloat16)
    return high, low


def mm(a, b):
    return jnp.dot(a, b, preferred_element_type=jnp.float32)


def exact_times(value, table):
    high, low = split(value)
    return mm(high, table) + mm(low, table)


def fft_leading(re, im, sign):
    count = len(re)
    if count == 1:
        return re, im
    if count == 2:
        return [re[0] + re[1], re[0] - re[1]], [im[0] + im[1], im[0] - im[1]]
    er, ei = fft_leading(re[0::2], im[0::2], sign)
    odr, odi = fft_leading(re[1::2], im[1::2], sign)
    half = count // 2
    out_r, out_i = [None] * count, [None] * count
    for k in range(half):
        angle = sign * 2.0 * np.pi * k / count
        c, s = float(np.cos(angle)), float(np.sin(angle))
        if k == 0:
            tr, ti = odr[k], odi[k]
        elif 4 * k == count:
            tr, ti = (-odi[k], odr[k]) if sign > 0 else (odi[k], -odr[k])
        else:
            tr = odr[k] * c - odi[k] * s
            ti = odr[k] * s + odi[k] * c
        out_r[k], out_i[k] = er[k] + tr, ei[k] + ti
        out_r[k + half], out_i[k + half] = er[k] - tr, ei[k] - ti
    return out_r, out_i


def weigh(spectra, table):
    rows, width = spectra.shape[0] // 2, spectra.shape[1]
    re, im = spectra[:rows], spectra[rows:]
    power = (re * re + im * im).astype(jnp.bfloat16)
    shape = (rows // PATCH, PATCH, width)
    near = mm(power, table("near_line")[:width, :width]).reshape(shape)
    level = jnp.sum(mm(power, table("level")[:width, :width]).reshape(shape), axis=1)
    scale = 1.0 / (9.0 * (level + 1e-06))
    weights = []
    for patch in range(rows // PATCH):
        value = near[patch]
        value = value + pltpu.roll(value, 1, 0) + pltpu.roll(value, PATCH - 1, 0)
        value = value * scale[patch : patch + 1] + BOX_FLOOR
        weights.append(value * lax.rsqrt(value))
    weight = jnp.concatenate(weights, axis=0)
    return jnp.concatenate([re * weight, im * weight], axis=0).astype(jnp.bfloat16)


def filter_dates(cells_ref, rims_ref, table, out_ref):
    dates, _, looks, gate_rows = out_ref.shape
    main = [cells_ref[date].astype(jnp.bfloat16) for date in range(dates)]
    rims = [rims_ref[pair].astype(jnp.bfloat16) for pair in range(dates // 2)]
    real, imag = [], []
    for date in range(dates):
        half = mm(jnp.concatenate([main[date], rims[date // 2]], axis=1), table("enter", date % 2)).astype(jnp.bfloat16)
        width = half.shape[1] // 2
        real.append(half[:, :width])
        imag.append(half[:, width:])
    half = mm(jnp.concatenate(main + rims, axis=1), table("extra")).astype(jnp.bfloat16)
    width = half.shape[1] // 2
    real.append(half[:, :width])
    imag.append(half[:, width:])
    groups = [(first, min(first + 2, dates + 1)) for first in range(0, dates + 1, 2)]
    spectra = []
    for first, last in groups:
        re, im = jnp.concatenate(real[first:last], axis=1), jnp.concatenate(imag[first:last], axis=1)
        spectra.append(mm(table("gate_fwd"), jnp.concatenate([re, im], axis=0)))
    weighted = [weigh(value, table) for value in spectra]
    image_re, image_im = [], []
    for (first, last), value in zip(groups, weighted):
        image = mm(table("gate_back"), value).astype(jnp.bfloat16)
        step = image.shape[1] // (last - first)
        for start in range(0, image.shape[1], step):
            image_re.append(image[:gate_rows, start : start + step])
            image_im.append(image[gate_rows:, start : start + step])
    contract = (((1,), (1,)), ((), ()))
    for date in range(dates):
        image = jnp.concatenate([image_re[date], image_im[date], image_re[dates], image_im[dates]], axis=1)
        result = lax.dot_general(table("line_back", date), image, contract, preferred_element_type=jnp.float32)
        out_ref[date, 0] = result[:looks]
        out_ref[date, 1] = result[looks:]


def chunk_gates(gates):
    return gates // 2 if gates % (2 * 4 * ML_RG) == 0 else gates


def stack_kernel(
    shards, places, offset_hbm, raw_hbm, filt_hbm, phase_hbm, pack_hbm, out_ref, pack, raw_ref, filt_ref, phase_ref,
    sent, columns, turned, trig, twid_ref, work, focused, looks_sent, looks_got, cells, rims, offset_ref, send_sem, recv_sem, load_sem,
):
    def table(name, index=0):
        first, height, panels, width = places[name]
        first += index * height * panels
        parts = [pack[first + i * height : first + (i + 1) * height, :] for i in range(panels)]
        whole = parts[0] if panels == 1 else jnp.concatenate(parts, axis=1)
        return whole[:, :width]

    dates, _, line_count, total_gates = raw_ref.shape
    chunks, pairs, _, block_rows, lanes = columns.shape
    gates = total_gates // shards
    part_gates = gates // chunks
    me = lax.axis_index("lines")

    loads = [
        pltpu.make_async_copy(source, target, load_sem.at[i])
        for i, (source, target) in enumerate(
            [(filt_hbm, filt_ref), (raw_hbm, raw_ref), (phase_hbm, phase_ref), (pack_hbm, pack), (offset_hbm, offset_ref)]
        )
    ]
    loads[0].start()
    loads[1].start()

    def ring(step):
        return lax.rem(me + step, shards)

    barrier = pltpu.get_barrier_semaphore()

    @pl.loop(1, shards)
    def _(step):
        pl.semaphore_signal(barrier, inc=1, device_id={"lines": ring(step)}, device_id_type=pl.DeviceIdType.MESH)

    for load in loads[2:]:
        load.start()

    def compress(chunk, pair):
        weights = filt_ref[...]
        if chunks > 1:
            weights = weights.reshape(2, shards, chunks, part_gates, total_gates)[:, :, chunk]
        weights = weights.reshape(2 * shards * part_gates, total_gates)
        half = shards * part_gates
        contract = (((1,), (1,)), ((), ()))
        for i in range(2):
            lines = raw_ref[2 * pair + i].reshape(2 * line_count, total_gates)
            product = lax.dot_general(weights, lines, contract, preferred_element_type=jnp.float32)
            real = product[:half, :line_count] - product[half:, line_count:]
            imag = product[half:, :line_count] + product[:half, line_count:]
            shape = (shards, part_gates, line_count)
            both = jnp.concatenate([real.reshape(shape), imag.reshape(shape)], axis=1)
            at = pl.ds(2 * i * part_gates, 2 * part_gates)
            sent[chunk, pair, :, at, :] = both.astype(jnp.bfloat16)

    def block(source, target, slot, peer):
        return pltpu.make_async_remote_copy(
            src_ref=source, dst_ref=target, send_sem=send_sem.at[slot], recv_sem=recv_sem.at[slot],
            device_id={"lines": peer}, device_id_type=pl.DeviceIdType.MESH,
        )

    def send_part(chunk, pair):
        slot = chunk * pairs + pair

        @pl.loop(1, shards)
        def _(step):
            peer = ring(step)
            block(sent.at[chunk, pair, peer], columns.at[chunk, pair, me], slot, peer).start()

        columns[chunk, pair, me] = sent[chunk, pair, me]

    def arrived(chunk, pair):
        part = pl.ds(0, shards - 1)
        slot = chunk * pairs + pair
        return block(sent.at[chunk, pair, part], columns.at[chunk, pair, part], slot, ring(1))

    def gathered(chunk):
        part = pl.ds(0, shards - 1)
        return block(looks_sent.at[chunk, part], looks_got.at[chunk, part], chunks * pairs + chunk, ring(1))

    loads[0].wait()
    loads[1].wait()
    for chunk in range(chunks):
        if chunk == 0:
            @pl.loop(0, pairs)
            def _(pair):
                compress(0, pair)

            pl.semaphore_wait(barrier, shards - 1)

            @pl.loop(0, pairs)
            def _(pair):
                send_part(0, pair)
        else:
            @pl.loop(0, pairs)
            def _(pair):
                compress(chunk, pair)
                send_part(chunk, pair)

    loads[2].wait()
    turned[...] = phase_ref[...].T

    @pl.loop(0, shards)
    def _(k):
        phase = turned[pl.ds(k, lanes, stride=shards), :].T
        at = pl.ds(pl.multiple_of(k * part_gates, part_gates), part_gates)
        cosine, sine = jnp.cos(phase), jnp.sin(phase)
        for chunk in range(chunks):
            trig[chunk, 0, at, :] = cosine[chunk * part_gates : (chunk + 1) * part_gates]
            trig[chunk, 1, at, :] = sine[chunk * part_gates : (chunk + 1) * part_gates]

    loads[3].wait()
    loads[4].wait()
    pieces = table("twiddle").astype(jnp.float32)
    count = twid_ref.shape[0]
    twid_ref[...] = pieces[:count] + pieces[count : 2 * count] + pieces[2 * count :]
    rows = shards * part_gates
    looks_rows = places["gate_sum"][1] // 3
    tile = looks_rows // shards

    @pl.loop(0, chunks)
    def _(chunk):
        @pl.loop(0, pairs)
        def _(pair):
            arrived(chunk, pair).wait_recv()
            for i in range(2):
                start = 2 * i * part_gates
                data = [
                    columns[chunk, pair, s, pl.ds(start, 2 * part_gates), :].astype(jnp.float32) for s in range(shards)
                ]
                for low in range(0, part_gates, 8):
                    re = [value[low : low + 8] for value in data]
                    im = [value[part_gates + low : part_gates + low + 8] for value in data]
                    re, im = fft_leading(re, im, -1.0)
                    for k in range(shards):
                        c, s = twid_ref[pl.ds(k, 1), :], twid_ref[pl.ds(shards + k, 1), :]
                        at = pl.ds(i * rows + k * part_gates + low, 8)
                        work[at, :lanes] = re[k] * c + im[k] * s
                        work[at, lanes:] = im[k] * c - re[k] * s
            spectrum = mm(work[...].astype(jnp.bfloat16), table("forward"))
            c, s = trig[chunk, 0], trig[chunk, 1]
            shifted = []
            for i in range(2):
                re, im = spectrum[i * rows : (i + 1) * rows, :lanes], spectrum[i * rows : (i + 1) * rows, lanes:]
                shifted.append(jnp.concatenate([re * c - im * s, re * s + im * c], axis=1))
            work[...] = mm(jnp.concatenate(shifted, axis=0).astype(jnp.bfloat16), table("backward"))
            for i in range(2):
                for low in range(0, part_gates, 8):
                    re, im = [], []
                    for k in range(shards):
                        c, s = twid_ref[pl.ds(k, 1), :], twid_ref[pl.ds(shards + k, 1), :]
                        at = pl.ds(i * rows + k * part_gates + low, 8)
                        a, b = work[at, :lanes], work[at, lanes:]
                        re.append(a * c - b * s)
                        im.append(b * c + a * s)
                    re, im = fft_leading(re, im, 1.0)
                    for n in range(shards):
                        at = pl.ds(n * part_gates + low, 8)
                        focused[2 * pair + i, at, :lanes] = re[n].astype(jnp.bfloat16).astype(jnp.float32)
                        focused[2 * pair + i, at, lanes:] = im[n].astype(jnp.bfloat16).astype(jnp.float32)

        joined = []
        for parity in range(2):
            parts = []
            for d in (parity, parity + 2):
                partner = lax.rem(d + offset_ref[d], dates)
                a, b = focused[d, :, :lanes], focused[d, :, lanes:]
                p, q = focused[partner, :, :lanes], focused[partner, :, lanes:]
                parts.append(jnp.concatenate([a * p + b * q, b * p - a * q], axis=1).astype(jnp.bfloat16))
            joined.append(jnp.concatenate(parts, axis=0))
        summed = [mm(table("gate_sum"), value).astype(jnp.bfloat16) for value in joined]
        pieces = [mm(value[:looks_rows], table("main")) for value in summed]
        sides = [jnp.concatenate([value[looks_rows : 2 * looks_rows], value[2 * looks_rows :]], axis=1) for value in summed]
        rim = mm(sides[0], table("rim", 0)) + mm(sides[1], table("rim", 1))
        shaped = [piece.reshape(shards, tile, lanes) for piece in pieces + [rim]]
        looks_sent[chunk] = jnp.concatenate(shaped, axis=1).astype(looks_sent.dtype)

        @pl.loop(1, shards)
        def _(step):
            peer = ring(step)
            block(looks_sent.at[chunk, peer], looks_got.at[chunk, me], chunks * pairs + chunk, peer).start()

        looks_got[chunk, me] = looks_sent[chunk, me]

    @pl.loop(0, chunks)
    def _(chunk):
        @pl.loop(0, pairs)
        def _(pair):
            arrived(chunk, pair).wait_send()

    part_looks = tile // 2
    for chunk in range(chunks):
        gathered(chunk).wait_recv()
        for shard in range(shards):
            received = looks_got[chunk, shard].astype(jnp.float32)
            at = pl.ds((shard * chunks + chunk) * part_looks, part_looks)
            for q in range(2):
                for parity in range(2):
                    low = parity * tile + q * part_looks
                    cells[2 * q + parity, at, :] = received[low : low + part_looks]
                low = 2 * tile + q * part_looks
                rims[q, at, :] = received[low : low + part_looks]

    filter_dates(cells, rims, table, out_ref)

    @pl.loop(0, chunks)
    def _(chunk):
        gathered(chunk).wait_send()


def focus_tables(shards, part_gates, lanes):
    total = shards * lanes
    k1, n2 = np.arange(shards), np.arange(lanes)
    angle = 2.0 * np.pi / total * (np.outer(k1, n2) % total)
    twiddle = np.stack([np.cos(angle), np.sin(angle)]).astype(np.float32)
    grid = np.exp(-2j * np.pi / lanes * (np.outer(n2, n2) % lanes))
    forward = right_block(grid)
    backward = right_block(np.conj(grid)) / total
    group = np.kron(np.eye(part_gates // ML_RG), np.ones((1, ML_RG)))
    gate_sum = []
    for shift in (0, -1, 1):
        spread = np.einsum("js,qr,lg->jqlrsg", np.eye(shards, k=shift), np.eye(2), group)
        gate_sum.append(spread.reshape(shards * 2 * group.shape[0], -1))
    gate_sum = np.concatenate(gate_sum)
    looks = lanes // ML_AZ
    pair = np.kron(np.eye(looks), np.ones((ML_AZ, 1))) / (ML_RG * ML_AZ)
    main = np.kron(np.eye(2), pair)
    rim = np.zeros((2, 4 * lanes, lanes))
    for parity in range(2):
        for part in range(2):
            low = parity * 4 * HALF + part * 2 * HALF
            source = part * lanes
            rim[parity, source : source + lanes, low : low + HALF] = pair[:, looks - HALF :]
            source += 2 * lanes
            rim[parity, source : source + lanes, low + HALF : low + 2 * HALF] = pair[:, :HALF]
    twiddle = twiddle.reshape(2 * shards, lanes)
    high = twiddle.astype(ml_dtypes.bfloat16).astype(np.float32)
    middle = (twiddle - high).astype(ml_dtypes.bfloat16).astype(np.float32)
    pieces = np.concatenate([high, middle, twiddle - high - middle])
    return {
        "twiddle": pieces, "forward": forward, "backward": backward, "gate_sum": gate_sum, "main": main, "rim": rim,
    }


def filtered_looks(raw_echo, range_filter, azimuth_phase, pair_offset, shards):
    dates, _, lanes, total_gates = raw_echo.shape
    gates = azimuth_phase.shape[0]
    part_gates = chunk_gates(gates)
    chunks, pairs = gates // part_gates, dates // 2
    gate_rows, looks = total_gates // ML_RG, lanes // ML_AZ
    tables = focus_tables(shards, part_gates, lanes)
    tables.update(filter_tables(gate_rows, looks, dates))
    places, pack = packed(tables)
    rows = shards * part_gates
    block = (chunks, shards, 6 * (part_gates // ML_RG), lanes)
    columns = (chunks, pairs, shards, 4 * part_gates, lanes)
    return pl.pallas_call(
        functools.partial(stack_kernel, shards, places),
        in_specs=[pl.BlockSpec(memory_space=pl.ANY)] * 5,
        out_specs=VMEM,
        out_shape=jax.ShapeDtypeStruct((dates, 2, looks, gate_rows), jnp.float32),
        scratch_shapes=[
            pltpu.VMEM(pack.shape, pack.dtype),
            pltpu.VMEM(raw_echo.shape, raw_echo.dtype),
            pltpu.VMEM(range_filter.shape, range_filter.dtype),
            pltpu.VMEM(azimuth_phase.shape, azimuth_phase.dtype),
            pltpu.VMEM(columns, jnp.bfloat16),
            pltpu.VMEM(columns, jnp.bfloat16),
            pltpu.VMEM(azimuth_phase.shape[::-1], jnp.float32),
            pltpu.VMEM((chunks, 2, rows, lanes), jnp.float32),
            pltpu.VMEM((2 * shards, lanes), jnp.float32),
            pltpu.VMEM((2 * rows, 2 * lanes), jnp.float32),
            pltpu.VMEM((dates, rows, 2 * lanes), jnp.float32),
            pltpu.VMEM(block, jnp.bfloat16),
            pltpu.VMEM(block, jnp.bfloat16),
            pltpu.VMEM((dates, gate_rows, 2 * looks), jnp.float32),
            pltpu.VMEM((pairs, gate_rows, 2 * looks), jnp.float32),
            pltpu.SMEM(pair_offset.shape, pair_offset.dtype),
            pltpu.SemaphoreType.DMA((chunks * (pairs + 1),)),
            pltpu.SemaphoreType.DMA((chunks * (pairs + 1),)),
            pltpu.SemaphoreType.DMA((5,)),
        ],
        compiler_params=pltpu.CompilerParams(collective_id=0, has_side_effects=True, vmem_limit_bytes=54784 * 1024),
        name="stack",
    )(pair_offset, raw_echo, range_filter, azimuth_phase, pack)


def tri_window():
    return 1.0 - np.abs(np.arange(PATCH) - (PATCH - 1) / 2.0) / HALF


def patch_maps(cells, starts):
    count = len(starts)
    forward = np.zeros((cells, count, PATCH), np.complex128)
    backward = np.zeros((count, PATCH, cells), np.complex128)
    window, k = tri_window(), np.arange(PATCH)
    for patch, start in enumerate(starts):
        for a in range(PATCH):
            cell = start + a
            if 0 <= cell < cells:
                wave = np.exp(2j * np.pi / PATCH * (k * a % PATCH))
                forward[cell, patch] = np.conj(wave)
                backward[patch, :, cell] = wave * window[a] / PATCH
    return forward.reshape(cells, -1), backward.reshape(-1, cells)


def filter_tables(gate_rows, looks, dates):
    gate_starts = range(-HALF, gate_rows - HALF + 1, HALF)
    line_starts = range(0, looks + 1, HALF)
    gate_fwd, gate_back = patch_maps(gate_rows, gate_starts)
    line_fwd, _ = patch_maps(looks + PATCH, line_starts)
    _, line_back = patch_maps(looks, [start - HALF for start in line_starts])
    width = (len(line_starts) - 1) * PATCH
    span = 2 * looks

    def entry(columns, main, low, table):
        block = right_block(columns).reshape(2, looks + PATCH, -1)
        for part in range(2):
            table[main + part * looks : main + (part + 1) * looks] += block[part, HALF : HALF + looks]
            at = low + part * 2 * HALF
            table[at : at + HALF] += block[part, :HALF]
            table[at + HALF : at + 2 * HALF] += block[part, HALF + looks :]

    enter = np.zeros((2, 2 * span, 2 * width))
    for parity in range(2):
        entry(line_fwd[:, :width], 0, span + parity * 4 * HALF, enter[parity])
    wide = dates * PATCH
    extra = np.zeros((dates * span + dates // 2 * span, 2 * wide))
    back = np.zeros((dates, 2 * looks, 2 * width + 2 * wide))
    for date in range(dates):
        placed = np.zeros((looks + PATCH, wide), np.complex128)
        placed[:, date * PATCH : (date + 1) * PATCH] = line_fwd[:, width:]
        entry(placed, date * span, dates * span + date // 2 * span + date % 2 * 4 * HALF, extra)
        placed = np.zeros((wide, looks), np.complex128)
        placed[date * PATCH : (date + 1) * PATCH] = line_back[width:]
        back[date, :, : 2 * width] = right_block(line_back[:width]).T
        back[date, :, 2 * width :] = right_block(placed).T
    gap = (np.arange(PATCH)[:, None] - np.arange(PATCH)[None, :]) % PATCH
    near = (gap <= 1) | (gap == PATCH - 1)
    group = max(2 * width, wide) // PATCH
    near_line = np.kron(np.eye(group), near)
    level = np.kron(np.eye(group), np.ones((PATCH, PATCH)) / PATCH**2)
    return {
        "enter": enter,
        "extra": extra,
        "gate_fwd": left_block(gate_fwd.T),
        "near_line": near_line,
        "level": level,
        "gate_back": left_block(gate_back.T),
        "line_back": back,
    }


def packed(tables):
    places, panels, first = {}, [], 0
    for name, table in tables.items():
        stack = table.reshape((-1,) + table.shape[-2:])
        _, height, width = stack.shape
        count = -(-width // LANES)
        places[name] = (first, height, count, width)
        for part in np.pad(stack, ((0, 0), (0, 0), (0, count * LANES - width))):
            for i in range(count):
                panels.append(part[:, i * LANES : (i + 1) * LANES])
                first += height
    return places, np.concatenate(panels).astype(ml_dtypes.bfloat16)


def body(raw_echo, range_filter, azimuth_phase, pair_offset):
    shards = lax.axis_size("lines")
    image = filtered_looks(raw_echo, range_filter, azimuth_phase, pair_offset, shards)
    return image.transpose(0, 1, 3, 2)


def solution(mesh):
    placed = (P("groups", None, "lines", None), P(), P("lines", None), P())
    return jax.shard_map(
        body,
        mesh=mesh,
        in_specs=placed,
        out_specs=P("groups", None, None, "lines"),
        check_vma=False,
    )
```

```python
import functools

import jax
import jax.numpy as jnp
import ml_dtypes
import numpy as np
from jax import lax
from jax.experimental import pallas as pl
from jax.experimental.pallas import tpu as pltpu
from jax.sharding import PartitionSpec as P

ML_RG = 4
ML_AZ = 2
PATCH = 32
HALF = PATCH // 2
BOX_FLOOR = 0.25
LANES = 128
VMEM = pl.BlockSpec(memory_space=pltpu.VMEM)


def right_block(table):
    return np.block([[table.real, table.imag], [-table.imag, table.real]])


def left_block(table):
    return np.block([[table.real, -table.imag], [table.imag, table.real]])


def split(value):
    high = value.astype(jnp.bfloat16)
    low = (value - high.astype(jnp.float32)).astype(jnp.bfloat16)
    return high, low


def mm(a, b):
    return jnp.dot(a, b, preferred_element_type=jnp.float32)


def exact_times(value, table):
    high, low = split(value)
    return mm(high, table) + mm(low, table)


def fft_leading(re, im, sign):
    count = len(re)
    if count == 1:
        return re, im
    if count == 2:
        return [re[0] + re[1], re[0] - re[1]], [im[0] + im[1], im[0] - im[1]]
    er, ei = fft_leading(re[0::2], im[0::2], sign)
    odr, odi = fft_leading(re[1::2], im[1::2], sign)
    half = count // 2
    out_r, out_i = [None] * count, [None] * count
    for k in range(half):
        angle = sign * 2.0 * np.pi * k / count
        c, s = float(np.cos(angle)), float(np.sin(angle))
        if k == 0:
            tr, ti = odr[k], odi[k]
        elif 4 * k == count:
            tr, ti = (-odi[k], odr[k]) if sign > 0 else (odi[k], -odr[k])
        else:
            tr = odr[k] * c - odi[k] * s
            ti = odr[k] * s + odi[k] * c
        out_r[k], out_i[k] = er[k] + tr, ei[k] + ti
        out_r[k + half], out_i[k + half] = er[k] - tr, ei[k] - ti
    return out_r, out_i


def weigh(spectra, table):
    rows, width = spectra.shape[0] // 2, spectra.shape[1]
    re, im = spectra[:rows], spectra[rows:]
    power = (re * re + im * im).astype(jnp.bfloat16)
    shape = (rows // PATCH, PATCH, width)
    near = mm(power, table("near_line")[:width, :width]).reshape(shape)
    level = jnp.sum(mm(power, table("level")[:width, :width]).reshape(shape), axis=1)
    scale = 1.0 / (9.0 * (level + 1e-06))
    weights = []
    for patch in range(rows // PATCH):
        value = near[patch]
        value = value + pltpu.roll(value, 1, 0) + pltpu.roll(value, PATCH - 1, 0)
        value = value * scale[patch : patch + 1] + BOX_FLOOR
        weights.append(value * lax.rsqrt(value))
    weight = jnp.concatenate(weights, axis=0)
    return jnp.concatenate([re * weight, im * weight], axis=0).astype(jnp.bfloat16)


def filter_dates(cells_ref, rims_ref, table, out_ref):
    dates, _, looks, gate_rows = out_ref.shape
    main = [cells_ref[date].astype(jnp.bfloat16) for date in range(dates)]
    rims = [rims_ref[pair].astype(jnp.bfloat16) for pair in range(dates // 2)]
    real, imag = [], []
    for date in range(dates):
        half = mm(jnp.concatenate([main[date], rims[date // 2]], axis=1), table("enter", date % 2)).astype(jnp.bfloat16)
        width = half.shape[1] // 2
        real.append(half[:, :width])
        imag.append(half[:, width:])
    half = mm(jnp.concatenate(main + rims, axis=1), table("extra")).astype(jnp.bfloat16)
    width = half.shape[1] // 2
    real.append(half[:, :width])
    imag.append(half[:, width:])
    groups = [(first, min(first + 2, dates + 1)) for first in range(0, dates + 1, 2)]
    spectra = []
    for first, last in groups:
        re, im = jnp.concatenate(real[first:last], axis=1), jnp.concatenate(imag[first:last], axis=1)
        spectra.append(mm(table("gate_fwd"), jnp.concatenate([re, im], axis=0)))
    weighted = [weigh(value, table) for value in spectra]
    image_re, image_im = [], []
    for (first, last), value in zip(groups, weighted):
        image = mm(table("gate_back"), value).astype(jnp.bfloat16)
        step = image.shape[1] // (last - first)
        for start in range(0, image.shape[1], step):
            image_re.append(image[:gate_rows, start : start + step])
            image_im.append(image[gate_rows:, start : start + step])
    contract = (((1,), (1,)), ((), ()))
    for date in range(dates):
        image = jnp.concatenate([image_re[date], image_im[date], image_re[dates], image_im[dates]], axis=1)
        result = lax.dot_general(table("line_back", date), image, contract, preferred_element_type=jnp.float32)
        out_ref[date, 0] = result[:looks]
        out_ref[date, 1] = result[looks:]


def chunk_gates(gates):
    return gates // 2 if gates % (2 * 4 * ML_RG) == 0 else gates


def stack_kernel(
    shards, places, offset_hbm, raw_hbm, filt_hbm, phase_hbm, pack_hbm, out_ref, pack, raw_ref, filt_ref, phase_ref,
    sent, columns, turned, trig, twid_ref, work, focused, looks_sent, looks_got, cells, rims, offset_ref, send_sem, recv_sem, load_sem,
):
    def table(name, index=0):
        first, height, panels, width = places[name]
        first += index * height * panels
        parts = [pack[first + i * height : first + (i + 1) * height, :] for i in range(panels)]
        whole = parts[0] if panels == 1 else jnp.concatenate(parts, axis=1)
        return whole[:, :width]

    dates, _, line_count, total_gates = raw_ref.shape
    chunks, pairs, _, block_rows, lanes = columns.shape
    gates = total_gates // shards
    part_gates = gates // chunks
    me = lax.axis_index("lines")

    loads = [
        pltpu.make_async_copy(source, target, load_sem.at[i])
        for i, (source, target) in enumerate(
            [(filt_hbm, filt_ref), (raw_hbm, raw_ref), (phase_hbm, phase_ref), (pack_hbm, pack), (offset_hbm, offset_ref)]
        )
    ]
    loads[0].start()
    loads[1].start()

    def ring(step):
        return lax.rem(me + step, shards)

    barrier = pltpu.get_barrier_semaphore()

    @pl.loop(1, shards)
    def _(step):
        pl.semaphore_signal(barrier, inc=1, device_id={"lines": ring(step)}, device_id_type=pl.DeviceIdType.MESH)

    for load in loads[2:]:
        load.start()

    def compress(chunk, pair):
        weights = filt_ref[...]
        if chunks > 1:
            weights = weights.reshape(2, shards, chunks, part_gates, total_gates)[:, :, chunk]
        weights = weights.reshape(2 * shards * part_gates, total_gates)
        half = shards * part_gates
        contract = (((1,), (1,)), ((), ()))
        for i in range(2):
            lines = raw_ref[2 * pair + i].reshape(2 * line_count, total_gates)
            product = lax.dot_general(weights, lines, contract, preferred_element_type=jnp.float32)
            real = product[:half, :line_count] - product[half:, line_count:]
            imag = product[half:, :line_count] + product[:half, line_count:]
            shape = (shards, part_gates, line_count)
            both = jnp.concatenate([real.reshape(shape), imag.reshape(shape)], axis=1)
            at = pl.ds(2 * i * part_gates, 2 * part_gates)
            sent[chunk, pair, :, at, :] = both.astype(jnp.bfloat16)

    def block(source, target, slot, peer):
        return pltpu.make_async_remote_copy(
            src_ref=source, dst_ref=target, send_sem=send_sem.at[slot], recv_sem=recv_sem.at[slot],
            device_id={"lines": peer}, device_id_type=pl.DeviceIdType.MESH,
        )

    def send_part(chunk, pair):
        slot = chunk * pairs + pair

        @pl.loop(1, shards)
        def _(step):
            peer = ring(step)
            block(sent.at[chunk, pair, peer], columns.at[chunk, pair, me], slot, peer).start()

        columns[chunk, pair, me] = sent[chunk, pair, me]

    def send_looks(chunk):
        @pl.loop(1, shards)
        def _(step):
            peer = ring(step)
            block(looks_sent.at[chunk, peer], looks_got.at[chunk, me], chunks * pairs + chunk, peer).start()

        looks_got[chunk, me] = looks_sent[chunk, me]

    def arrived(chunk, pair):
        part = pl.ds(0, shards - 1)
        slot = chunk * pairs + pair
        return block(sent.at[chunk, pair, part], columns.at[chunk, pair, part], slot, ring(1))

    def gathered(chunk):
        part = pl.ds(0, shards - 1)
        return block(looks_sent.at[chunk, part], looks_got.at[chunk, part], chunks * pairs + chunk, ring(1))

    loads[0].wait()
    loads[1].wait()
    for chunk in range(chunks):
        if chunk == 0:
            @pl.loop(0, pairs)
            def _(pair):
                compress(0, pair)

            pl.semaphore_wait(barrier, shards - 1)

            @pl.loop(0, pairs)
            def _(pair):
                send_part(0, pair)
        else:
            @pl.loop(0, pairs)
            def _(pair):
                compress(chunk, pair)
                send_part(chunk, pair)

    loads[2].wait()
    turned[...] = phase_ref[...].T

    @pl.loop(0, shards)
    def _(k):
        phase = turned[pl.ds(k, lanes, stride=shards), :].T
        at = pl.ds(pl.multiple_of(k * part_gates, part_gates), part_gates)
        cosine, sine = jnp.cos(phase), jnp.sin(phase)
        for chunk in range(chunks):
            trig[chunk, 0, at, :] = cosine[chunk * part_gates : (chunk + 1) * part_gates]
            trig[chunk, 1, at, :] = sine[chunk * part_gates : (chunk + 1) * part_gates]

    loads[3].wait()
    loads[4].wait()
    pieces = table("twiddle").astype(jnp.float32)
    count = twid_ref.shape[0]
    twid_ref[...] = pieces[:count] + pieces[count : 2 * count] + pieces[2 * count :]
    rows = shards * part_gates
    looks_rows = places["gate_sum"][1] // 3
    tile = looks_rows // shards

    @pl.loop(0, chunks)
    def _(chunk):
        @pl.loop(0, pairs)
        def _(pair):
            arrived(chunk, pair).wait_recv()

            @pl.when((chunk > 0) & (pair == pairs - 1))
            def _():
                send_looks(chunk - 1)

            for i in range(2):
                start = 2 * i * part_gates
                data = [
                    columns[chunk, pair, s, pl.ds(start, 2 * part_gates), :].astype(jnp.float32) for s in range(shards)
                ]
                for low in range(0, part_gates, 8):
                    re = [value[low : low + 8] for value in data]
                    im = [value[part_gates + low : part_gates + low + 8] for value in data]
                    re, im = fft_leading(re, im, -1.0)
                    for k in range(shards):
                        c, s = twid_ref[pl.ds(k, 1), :], twid_ref[pl.ds(shards + k, 1), :]
                        at = pl.ds(i * rows + k * part_gates + low, 8)
                        work[at, :lanes] = re[k] * c + im[k] * s
                        work[at, lanes:] = im[k] * c - re[k] * s
            spectrum = mm(work[...].astype(jnp.bfloat16), table("forward"))
            c, s = trig[chunk, 0], trig[chunk, 1]
            shifted = []
            for i in range(2):
                re, im = spectrum[i * rows : (i + 1) * rows, :lanes], spectrum[i * rows : (i + 1) * rows, lanes:]
                shifted.append(jnp.concatenate([re * c - im * s, re * s + im * c], axis=1))
            work[...] = mm(jnp.concatenate(shifted, axis=0).astype(jnp.bfloat16), table("backward"))
            for i in range(2):
                for low in range(0, part_gates, 8):
                    re, im = [], []
                    for k in range(shards):
                        c, s = twid_ref[pl.ds(k, 1), :], twid_ref[pl.ds(shards + k, 1), :]
                        at = pl.ds(i * rows + k * part_gates + low, 8)
                        a, b = work[at, :lanes], work[at, lanes:]
                        re.append(a * c - b * s)
                        im.append(b * c + a * s)
                    re, im = fft_leading(re, im, 1.0)
                    for n in range(shards):
                        at = pl.ds(n * part_gates + low, 8)
                        focused[2 * pair + i, at, :lanes] = re[n].astype(jnp.bfloat16).astype(jnp.float32)
                        focused[2 * pair + i, at, lanes:] = im[n].astype(jnp.bfloat16).astype(jnp.float32)

        joined = []
        for parity in range(2):
            parts = []
            for d in (parity, parity + 2):
                partner = lax.rem(d + offset_ref[d], dates)
                a, b = focused[d, :, :lanes], focused[d, :, lanes:]
                p, q = focused[partner, :, :lanes], focused[partner, :, lanes:]
                parts.append(jnp.concatenate([a * p + b * q, b * p - a * q], axis=1).astype(jnp.bfloat16))
            joined.append(jnp.concatenate(parts, axis=0))
        summed = [mm(table("gate_sum"), value).astype(jnp.bfloat16) for value in joined]
        pieces = [mm(value[:looks_rows], table("main")) for value in summed]
        sides = [jnp.concatenate([value[looks_rows : 2 * looks_rows], value[2 * looks_rows :]], axis=1) for value in summed]
        rim = mm(sides[0], table("rim", 0)) + mm(sides[1], table("rim", 1))
        shaped = [piece.reshape(shards, tile, lanes) for piece in pieces + [rim]]
        looks_sent[chunk] = jnp.concatenate(shaped, axis=1).astype(looks_sent.dtype)

        @pl.when(chunk == chunks - 1)
        def _():
            send_looks(chunk)

    @pl.loop(0, chunks)
    def _(chunk):
        @pl.loop(0, pairs)
        def _(pair):
            arrived(chunk, pair).wait_send()

    part_looks = tile // 2
    for chunk in range(chunks):
        gathered(chunk).wait_recv()
        for shard in range(shards):
            received = looks_got[chunk, shard].astype(jnp.float32)
            at = pl.ds((shard * chunks + chunk) * part_looks, part_looks)
            for q in range(2):
                for parity in range(2):
                    low = parity * tile + q * part_looks
                    cells[2 * q + parity, at, :] = received[low : low + part_looks]
                low = 2 * tile + q * part_looks
                rims[q, at, :] = received[low : low + part_looks]

    filter_dates(cells, rims, table, out_ref)

    @pl.loop(0, chunks)
    def _(chunk):
        gathered(chunk).wait_send()


def focus_tables(shards, part_gates, lanes):
    total = shards * lanes
    k1, n2 = np.arange(shards), np.arange(lanes)
    angle = 2.0 * np.pi / total * (np.outer(k1, n2) % total)
    twiddle = np.stack([np.cos(angle), np.sin(angle)]).astype(np.float32)
    grid = np.exp(-2j * np.pi / lanes * (np.outer(n2, n2) % lanes))
    forward = right_block(grid)
    backward = right_block(np.conj(grid)) / total
    group = np.kron(np.eye(part_gates // ML_RG), np.ones((1, ML_RG)))
    gate_sum = []
    for shift in (0, -1, 1):
        spread = np.einsum("js,qr,lg->jqlrsg", np.eye(shards, k=shift), np.eye(2), group)
        gate_sum.append(spread.reshape(shards * 2 * group.shape[0], -1))
    gate_sum = np.concatenate(gate_sum)
    looks = lanes // ML_AZ
    pair = np.kron(np.eye(looks), np.ones((ML_AZ, 1))) / (ML_RG * ML_AZ)
    main = np.kron(np.eye(2), pair)
    rim = np.zeros((2, 4 * lanes, lanes))
    for parity in range(2):
        for part in range(2):
            low = parity * 4 * HALF + part * 2 * HALF
            source = part * lanes
            rim[parity, source : source + lanes, low : low + HALF] = pair[:, looks - HALF :]
            source += 2 * lanes
            rim[parity, source : source + lanes, low + HALF : low + 2 * HALF] = pair[:, :HALF]
    twiddle = twiddle.reshape(2 * shards, lanes)
    high = twiddle.astype(ml_dtypes.bfloat16).astype(np.float32)
    middle = (twiddle - high).astype(ml_dtypes.bfloat16).astype(np.float32)
    pieces = np.concatenate([high, middle, twiddle - high - middle])
    return {
        "twiddle": pieces, "forward": forward, "backward": backward, "gate_sum": gate_sum, "main": main, "rim": rim,
    }


def filtered_looks(raw_echo, range_filter, azimuth_phase, pair_offset, shards):
    dates, _, lanes, total_gates = raw_echo.shape
    gates = azimuth_phase.shape[0]
    part_gates = chunk_gates(gates)
    chunks, pairs = gates // part_gates, dates // 2
    gate_rows, looks = total_gates // ML_RG, lanes // ML_AZ
    tables = focus_tables(shards, part_gates, lanes)
    tables.update(filter_tables(gate_rows, looks, dates))
    places, pack = packed(tables)
    rows = shards * part_gates
    block = (chunks, shards, 6 * (part_gates // ML_RG), lanes)
    columns = (chunks, pairs, shards, 4 * part_gates, lanes)
    return pl.pallas_call(
        functools.partial(stack_kernel, shards, places),
        in_specs=[pl.BlockSpec(memory_space=pl.ANY)] * 5,
        out_specs=VMEM,
        out_shape=jax.ShapeDtypeStruct((dates, 2, looks, gate_rows), jnp.float32),
        scratch_shapes=[
            pltpu.VMEM(pack.shape, pack.dtype),
            pltpu.VMEM(raw_echo.shape, raw_echo.dtype),
            pltpu.VMEM(range_filter.shape, range_filter.dtype),
            pltpu.VMEM(azimuth_phase.shape, azimuth_phase.dtype),
            pltpu.VMEM(columns, jnp.bfloat16),
            pltpu.VMEM(columns, jnp.bfloat16),
            pltpu.VMEM(azimuth_phase.shape[::-1], jnp.float32),
            pltpu.VMEM((chunks, 2, rows, lanes), jnp.float32),
            pltpu.VMEM((2 * shards, lanes), jnp.float32),
            pltpu.VMEM((2 * rows, 2 * lanes), jnp.float32),
            pltpu.VMEM((dates, rows, 2 * lanes), jnp.float32),
            pltpu.VMEM(block, jnp.bfloat16),
            pltpu.VMEM(block, jnp.bfloat16),
            pltpu.VMEM((dates, gate_rows, 2 * looks), jnp.float32),
            pltpu.VMEM((pairs, gate_rows, 2 * looks), jnp.float32),
            pltpu.SMEM(pair_offset.shape, pair_offset.dtype),
            pltpu.SemaphoreType.DMA((chunks * (pairs + 1),)),
            pltpu.SemaphoreType.DMA((chunks * (pairs + 1),)),
            pltpu.SemaphoreType.DMA((5,)),
        ],
        compiler_params=pltpu.CompilerParams(collective_id=0, has_side_effects=True, vmem_limit_bytes=54784 * 1024),
        name="stack",
    )(pair_offset, raw_echo, range_filter, azimuth_phase, pack)


def tri_window():
    return 1.0 - np.abs(np.arange(PATCH) - (PATCH - 1) / 2.0) / HALF


def patch_maps(cells, starts):
    count = len(starts)
    forward = np.zeros((cells, count, PATCH), np.complex128)
    backward = np.zeros((count, PATCH, cells), np.complex128)
    window, k = tri_window(), np.arange(PATCH)
    for patch, start in enumerate(starts):
        for a in range(PATCH):
            cell = start + a
            if 0 <= cell < cells:
                wave = np.exp(2j * np.pi / PATCH * (k * a % PATCH))
                forward[cell, patch] = np.conj(wave)
                backward[patch, :, cell] = wave * window[a] / PATCH
    return forward.reshape(cells, -1), backward.reshape(-1, cells)


def filter_tables(gate_rows, looks, dates):
    gate_starts = range(-HALF, gate_rows - HALF + 1, HALF)
    line_starts = range(0, looks + 1, HALF)
    gate_fwd, gate_back = patch_maps(gate_rows, gate_starts)
    line_fwd, _ = patch_maps(looks + PATCH, line_starts)
    _, line_back = patch_maps(looks, [start - HALF for start in line_starts])
    width = (len(line_starts) - 1) * PATCH
    span = 2 * looks

    def entry(columns, main, low, table):
        block = right_block(columns).reshape(2, looks + PATCH, -1)
        for part in range(2):
            table[main + part * looks : main + (part + 1) * looks] += block[part, HALF : HALF + looks]
            at = low + part * 2 * HALF
            table[at : at + HALF] += block[part, :HALF]
            table[at + HALF : at + 2 * HALF] += block[part, HALF + looks :]

    enter = np.zeros((2, 2 * span, 2 * width))
    for parity in range(2):
        entry(line_fwd[:, :width], 0, span + parity * 4 * HALF, enter[parity])
    wide = dates * PATCH
    extra = np.zeros((dates * span + dates // 2 * span, 2 * wide))
    back = np.zeros((dates, 2 * looks, 2 * width + 2 * wide))
    for date in range(dates):
        placed = np.zeros((looks + PATCH, wide), np.complex128)
        placed[:, date * PATCH : (date + 1) * PATCH] = line_fwd[:, width:]
        entry(placed, date * span, dates * span + date // 2 * span + date % 2 * 4 * HALF, extra)
        placed = np.zeros((wide, looks), np.complex128)
        placed[date * PATCH : (date + 1) * PATCH] = line_back[width:]
        back[date, :, : 2 * width] = right_block(line_back[:width]).T
        back[date, :, 2 * width :] = right_block(placed).T
    gap = (np.arange(PATCH)[:, None] - np.arange(PATCH)[None, :]) % PATCH
    near = (gap <= 1) | (gap == PATCH - 1)
    group = max(2 * width, wide) // PATCH
    near_line = np.kron(np.eye(group), near)
    level = np.kron(np.eye(group), np.ones((PATCH, PATCH)) / PATCH**2)
    return {
        "enter": enter,
        "extra": extra,
        "gate_fwd": left_block(gate_fwd.T),
        "near_line": near_line,
        "level": level,
        "gate_back": left_block(gate_back.T),
        "line_back": back,
    }


def packed(tables):
    places, panels, first = {}, [], 0
    for name, table in tables.items():
        stack = table.reshape((-1,) + table.shape[-2:])
        _, height, width = stack.shape
        count = -(-width // LANES)
        places[name] = (first, height, count, width)
        for part in np.pad(stack, ((0, 0), (0, 0), (0, count * LANES - width))):
            for i in range(count):
                panels.append(part[:, i * LANES : (i + 1) * LANES])
                first += height
    return places, np.concatenate(panels).astype(ml_dtypes.bfloat16)


def body(raw_echo, range_filter, azimuth_phase, pair_offset):
    shards = lax.axis_size("lines")
    image = filtered_looks(raw_echo, range_filter, azimuth_phase, pair_offset, shards)
    return image.transpose(0, 1, 3, 2)


def solution(mesh):
    placed = (P("groups", None, "lines", None), P(), P("lines", None), P())
    return jax.shard_map(
        body,
        mesh=mesh,
        in_specs=placed,
        out_specs=P("groups", None, None, "lines"),
        check_vma=False,
    )
```

```python
import functools

import jax
import jax.numpy as jnp
import ml_dtypes
import numpy as np
from jax import lax
from jax.experimental import pallas as pl
from jax.experimental.pallas import tpu as pltpu
from jax.sharding import PartitionSpec as P

ML_RG = 4
ML_AZ = 2
PATCH = 32
HALF = PATCH // 2
BOX_FLOOR = 0.25
LANES = 128
VMEM = pl.BlockSpec(memory_space=pltpu.VMEM)


def right_block(table):
    return np.block([[table.real, table.imag], [-table.imag, table.real]])


def left_block(table):
    return np.block([[table.real, -table.imag], [table.imag, table.real]])


def split(value):
    high = value.astype(jnp.bfloat16)
    low = (value - high.astype(jnp.float32)).astype(jnp.bfloat16)
    return high, low


def mm(a, b):
    return jnp.dot(a, b, preferred_element_type=jnp.float32)


def exact_times(value, table):
    high, low = split(value)
    return mm(high, table) + mm(low, table)


def fft_leading(re, im, sign):
    count = len(re)
    if count == 1:
        return re, im
    if count == 2:
        return [re[0] + re[1], re[0] - re[1]], [im[0] + im[1], im[0] - im[1]]
    er, ei = fft_leading(re[0::2], im[0::2], sign)
    odr, odi = fft_leading(re[1::2], im[1::2], sign)
    half = count // 2
    out_r, out_i = [None] * count, [None] * count
    for k in range(half):
        angle = sign * 2.0 * np.pi * k / count
        c, s = float(np.cos(angle)), float(np.sin(angle))
        if k == 0:
            tr, ti = odr[k], odi[k]
        elif 4 * k == count:
            tr, ti = (-odi[k], odr[k]) if sign > 0 else (odi[k], -odr[k])
        else:
            tr = odr[k] * c - odi[k] * s
            ti = odr[k] * s + odi[k] * c
        out_r[k], out_i[k] = er[k] + tr, ei[k] + ti
        out_r[k + half], out_i[k + half] = er[k] - tr, ei[k] - ti
    return out_r, out_i


def weigh(spectra, table):
    rows, width = spectra.shape[0] // 2, spectra.shape[1]
    re, im = spectra[:rows], spectra[rows:]
    power = (re * re + im * im).astype(jnp.bfloat16)
    shape = (rows // PATCH, PATCH, width)
    near = mm(power, table("near_line")[:width, :width]).reshape(shape)
    level = jnp.sum(mm(power, table("level")[:width, :width]).reshape(shape), axis=1)
    scale = 1.0 / (9.0 * (level + 1e-06))
    weights = []
    for patch in range(rows // PATCH):
        value = near[patch]
        value = value + pltpu.roll(value, 1, 0) + pltpu.roll(value, PATCH - 1, 0)
        value = value * scale[patch : patch + 1] + BOX_FLOOR
        weights.append(value * lax.rsqrt(value))
    weight = jnp.concatenate(weights, axis=0)
    return jnp.concatenate([re * weight, im * weight], axis=0).astype(jnp.bfloat16)


def filter_dates(cells_ref, rims_ref, table, out_ref):
    dates, _, looks, gate_rows = out_ref.shape
    main = [cells_ref[date].astype(jnp.bfloat16) for date in range(dates)]
    rims = [rims_ref[pair].astype(jnp.bfloat16) for pair in range(dates // 2)]
    real, imag = [], []
    for date in range(dates):
        half = mm(jnp.concatenate([main[date], rims[date // 2]], axis=1), table("enter", date % 2)).astype(jnp.bfloat16)
        width = half.shape[1] // 2
        real.append(half[:, :width])
        imag.append(half[:, width:])
    half = mm(jnp.concatenate(main + rims, axis=1), table("extra")).astype(jnp.bfloat16)
    width = half.shape[1] // 2
    real.append(half[:, :width])
    imag.append(half[:, width:])
    groups = [(first, min(first + 2, dates + 1)) for first in range(0, dates + 1, 2)]
    spectra = []
    for first, last in groups:
        re, im = jnp.concatenate(real[first:last], axis=1), jnp.concatenate(imag[first:last], axis=1)
        spectra.append(mm(table("gate_fwd"), jnp.concatenate([re, im], axis=0)))
    weighted = [weigh(value, table) for value in spectra]
    image_re, image_im = [], []
    for (first, last), value in zip(groups, weighted):
        image = mm(table("gate_back"), value).astype(jnp.bfloat16)
        step = image.shape[1] // (last - first)
        for start in range(0, image.shape[1], step):
            image_re.append(image[:gate_rows, start : start + step])
            image_im.append(image[gate_rows:, start : start + step])
    contract = (((1,), (1,)), ((), ()))
    for date in range(dates):
        image = jnp.concatenate([image_re[date], image_im[date], image_re[dates], image_im[dates]], axis=1)
        result = lax.dot_general(table("line_back", date), image, contract, preferred_element_type=jnp.float32)
        out_ref[date, 0] = result[:looks]
        out_ref[date, 1] = result[looks:]


def chunk_gates(gates):
    return gates // 2 if gates % (2 * 4 * ML_RG) == 0 else gates


def stack_kernel(
    shards, places, offset_hbm, raw_hbm, filt_hbm, phase_hbm, pack_hbm, out_ref, pack, raw_ref, filt_ref, phase_ref,
    sent, columns, turned, trig, twid_ref, work, focused, looks_sent, looks_got, cells, rims, offset_ref, send_sem, recv_sem, load_sem, relay_sem,
):
    def table(name, index=0):
        first, height, panels, width = places[name]
        first += index * height * panels
        parts = [pack[first + i * height : first + (i + 1) * height, :] for i in range(panels)]
        whole = parts[0] if panels == 1 else jnp.concatenate(parts, axis=1)
        return whole[:, :width]

    dates, _, line_count, total_gates = raw_ref.shape
    chunks, pairs, _, block_rows, lanes = columns.shape
    gates = total_gates // shards
    part_gates = gates // chunks
    me = lax.axis_index("lines")

    loads = [
        pltpu.make_async_copy(source, target, load_sem.at[i])
        for i, (source, target) in enumerate(
            [(filt_hbm, filt_ref), (raw_hbm, raw_ref), (phase_hbm, phase_ref), (pack_hbm, pack), (offset_hbm, offset_ref)]
        )
    ]
    loads[0].start()
    loads[1].start()

    def ring(step):
        return lax.rem(me + step, shards)

    barrier = pltpu.get_barrier_semaphore()

    def signal(sem, peer):
        pl.semaphore_signal(sem, inc=1, device_id={"lines": peer}, device_id_type=pl.DeviceIdType.MESH)

    quarter = shards // 4
    mine = me // quarter
    outer = (mine == 0) | (mine == 3)
    opposite = lax.rem(mine + 2, 4)

    def is_near(peer):
        place = peer // quarter
        return (place != opposite) & jnp.logical_not(outer & (place == 3 - mine))

    @pl.loop(1, shards)
    def _(step):
        peer = ring(step)

        @pl.when(is_near(peer))
        def _():
            signal(barrier, peer)


    def compress(chunk, pair):
        weights = filt_ref[...]
        if chunks > 1:
            weights = weights.reshape(2, shards, chunks, part_gates, total_gates)[:, :, chunk]
        weights = weights.reshape(2 * shards * part_gates, total_gates)
        half = shards * part_gates
        contract = (((1,), (1,)), ((), ()))
        for i in range(2):
            lines = raw_ref[2 * pair + i].reshape(2 * line_count, total_gates)
            product = lax.dot_general(weights, lines, contract, preferred_element_type=jnp.float32)
            real = product[:half, :line_count] - product[half:, line_count:]
            imag = product[half:, :line_count] + product[:half, line_count:]
            shape = (shards, part_gates, line_count)
            both = jnp.concatenate([real.reshape(shape), imag.reshape(shape)], axis=1)
            at = pl.ds(2 * i * part_gates, 2 * part_gates)
            sent[chunk, pair, :, at, :] = both.astype(jnp.bfloat16)

    def block(source, target, slot, peer):
        return pltpu.make_async_remote_copy(
            src_ref=source, dst_ref=target, send_sem=send_sem.at[slot], recv_sem=recv_sem.at[slot],
            device_id={"lines": peer}, device_id_type=pl.DeviceIdType.MESH,
        )

    def send_block(chunk, pair, peer):
        block(sent.at[chunk, pair, peer], columns.at[chunk, pair, me], chunk * pairs + pair, peer).start()

    def send_part(chunk, pair):
        @pl.loop(1, shards)
        def _(step):
            send_block(chunk, pair, ring(step))

        columns[chunk, pair, me] = sent[chunk, pair, me]

    def send_looks(chunk):
        @pl.loop(1, shards)
        def _(step):
            peer = ring(step)
            block(looks_sent.at[chunk, peer], looks_got.at[chunk, me], chunks * pairs + chunk, peer).start()

        looks_got[chunk, me] = looks_sent[chunk, me]

    def arrived(chunk, pair):
        part = pl.ds(0, shards - 1)
        slot = chunk * pairs + pair
        return block(sent.at[chunk, pair, part], columns.at[chunk, pair, part], slot, ring(1))

    def gathered(chunk):
        part = pl.ds(0, shards - 1)
        return block(looks_sent.at[chunk, part], looks_got.at[chunk, part], chunks * pairs + chunk, ring(1))

    loads[0].wait()
    loads[1].wait()
    for load in loads[2:]:
        load.start()
    for chunk in range(chunks):
        if chunk == 0:
            compress(0, 0)
            pl.semaphore_wait(barrier, jnp.where(outer, 2 * quarter - 1, 3 * quarter - 1))

            @pl.when(jnp.logical_not(outer))
            def _():
                signal(relay_sem.at[0], me - quarter)
                signal(relay_sem.at[1], me + quarter)

            @pl.loop(1, shards)
            def _(step):
                peer = ring(step)

                @pl.when(is_near(peer))
                def _():
                    send_block(0, 0, peer)

            @pl.when(mine < 2)
            def _():
                pl.semaphore_wait(relay_sem.at[0], 1)

            @pl.when(mine >= 2)
            def _():
                pl.semaphore_wait(relay_sem.at[1], 1)

            @pl.when(mine == 1)
            def _():
                signal(relay_sem.at[2], me - quarter)

            @pl.when(mine == 2)
            def _():
                signal(relay_sem.at[2], me + quarter)

            @pl.loop(0, quarter)
            def _(step):
                send_block(0, 0, opposite * quarter + step)

            @pl.loop(1, pairs)
            def _(pair):
                compress(0, pair)

            @pl.when(outer)
            def _():
                pl.semaphore_wait(relay_sem.at[2], 1)

                @pl.loop(0, quarter)
                def _(step):
                    send_block(0, 0, (3 - mine) * quarter + step)

            columns[0, 0, me] = sent[0, 0, me]

            @pl.loop(1, pairs)
            def _(pair):
                send_part(0, pair)
        else:
            @pl.loop(0, pairs)
            def _(pair):
                compress(chunk, pair)
                send_part(chunk, pair)

    loads[2].wait()
    turned[...] = phase_ref[...].T

    @pl.loop(0, shards)
    def _(k):
        phase = turned[pl.ds(k, lanes, stride=shards), :].T
        at = pl.ds(pl.multiple_of(k * part_gates, part_gates), part_gates)
        cosine, sine = jnp.cos(phase), jnp.sin(phase)
        for chunk in range(chunks):
            trig[chunk, 0, at, :] = cosine[chunk * part_gates : (chunk + 1) * part_gates]
            trig[chunk, 1, at, :] = sine[chunk * part_gates : (chunk + 1) * part_gates]

    loads[3].wait()
    loads[4].wait()
    pieces = table("twiddle").astype(jnp.float32)
    count = twid_ref.shape[0]
    twid_ref[...] = pieces[:count] + pieces[count : 2 * count] + pieces[2 * count :]
    rows = shards * part_gates
    looks_rows = places["gate_sum"][1] // 3
    tile = looks_rows // shards

    @pl.loop(0, chunks)
    def _(chunk):
        @pl.loop(0, pairs)
        def _(pair):
            arrived(chunk, pair).wait_recv()

            @pl.when((chunk > 0) & (pair == pairs - 1))
            def _():
                send_looks(chunk - 1)

            for i in range(2):
                start = 2 * i * part_gates
                data = [
                    columns[chunk, pair, s, pl.ds(start, 2 * part_gates), :].astype(jnp.float32) for s in range(shards)
                ]
                for low in range(0, part_gates, 8):
                    re = [value[low : low + 8] for value in data]
                    im = [value[part_gates + low : part_gates + low + 8] for value in data]
                    re, im = fft_leading(re, im, -1.0)
                    for k in range(shards):
                        c, s = twid_ref[pl.ds(k, 1), :], twid_ref[pl.ds(shards + k, 1), :]
                        at = pl.ds(i * rows + k * part_gates + low, 8)
                        work[at, :lanes] = re[k] * c + im[k] * s
                        work[at, lanes:] = im[k] * c - re[k] * s
            spectrum = mm(work[...].astype(jnp.bfloat16), table("forward"))
            c, s = trig[chunk, 0], trig[chunk, 1]
            shifted = []
            for i in range(2):
                re, im = spectrum[i * rows : (i + 1) * rows, :lanes], spectrum[i * rows : (i + 1) * rows, lanes:]
                shifted.append(jnp.concatenate([re * c - im * s, re * s + im * c], axis=1))
            work[...] = mm(jnp.concatenate(shifted, axis=0).astype(jnp.bfloat16), table("backward"))
            for i in range(2):
                for low in range(0, part_gates, 8):
                    re, im = [], []
                    for k in range(shards):
                        c, s = twid_ref[pl.ds(k, 1), :], twid_ref[pl.ds(shards + k, 1), :]
                        at = pl.ds(i * rows + k * part_gates + low, 8)
                        a, b = work[at, :lanes], work[at, lanes:]
                        re.append(a * c - b * s)
                        im.append(b * c + a * s)
                    re, im = fft_leading(re, im, 1.0)
                    for n in range(shards):
                        at = pl.ds(n * part_gates + low, 8)
                        focused[2 * pair + i, at, :lanes] = re[n].astype(jnp.bfloat16).astype(jnp.float32)
                        focused[2 * pair + i, at, lanes:] = im[n].astype(jnp.bfloat16).astype(jnp.float32)

        joined = []
        for parity in range(2):
            parts = []
            for d in (parity, parity + 2):
                partner = lax.rem(d + offset_ref[d], dates)
                a, b = focused[d, :, :lanes], focused[d, :, lanes:]
                p, q = focused[partner, :, :lanes], focused[partner, :, lanes:]
                parts.append(jnp.concatenate([a * p + b * q, b * p - a * q], axis=1).astype(jnp.bfloat16))
            joined.append(jnp.concatenate(parts, axis=0))
        summed = [mm(table("gate_sum"), value).astype(jnp.bfloat16) for value in joined]
        pieces = [mm(value[:looks_rows], table("main")) for value in summed]
        sides = [jnp.concatenate([value[looks_rows : 2 * looks_rows], value[2 * looks_rows :]], axis=1) for value in summed]
        rim = mm(sides[0], table("rim", 0)) + mm(sides[1], table("rim", 1))
        shaped = [piece.reshape(shards, tile, lanes) for piece in pieces + [rim]]
        looks_sent[chunk] = jnp.concatenate(shaped, axis=1).astype(looks_sent.dtype)

        @pl.when(chunk == chunks - 1)
        def _():
            send_looks(chunk)

    @pl.loop(0, chunks)
    def _(chunk):
        @pl.loop(0, pairs)
        def _(pair):
            arrived(chunk, pair).wait_send()

    part_looks = tile // 2
    for chunk in range(chunks):
        gathered(chunk).wait_recv()
        for shard in range(shards):
            received = looks_got[chunk, shard].astype(jnp.float32)
            at = pl.ds((shard * chunks + chunk) * part_looks, part_looks)
            for q in range(2):
                for parity in range(2):
                    low = parity * tile + q * part_looks
                    cells[2 * q + parity, at, :] = received[low : low + part_looks]
                low = 2 * tile + q * part_looks
                rims[q, at, :] = received[low : low + part_looks]

    filter_dates(cells, rims, table, out_ref)

    @pl.loop(0, chunks)
    def _(chunk):
        gathered(chunk).wait_send()


def focus_tables(shards, part_gates, lanes):
    total = shards * lanes
    k1, n2 = np.arange(shards), np.arange(lanes)
    angle = 2.0 * np.pi / total * (np.outer(k1, n2) % total)
    twiddle = np.stack([np.cos(angle), np.sin(angle)]).astype(np.float32)
    grid = np.exp(-2j * np.pi / lanes * (np.outer(n2, n2) % lanes))
    forward = right_block(grid)
    backward = right_block(np.conj(grid)) / total
    group = np.kron(np.eye(part_gates // ML_RG), np.ones((1, ML_RG)))
    gate_sum = []
    for shift in (0, -1, 1):
        spread = np.einsum("js,qr,lg->jqlrsg", np.eye(shards, k=shift), np.eye(2), group)
        gate_sum.append(spread.reshape(shards * 2 * group.shape[0], -1))
    gate_sum = np.concatenate(gate_sum)
    looks = lanes // ML_AZ
    pair = np.kron(np.eye(looks), np.ones((ML_AZ, 1))) / (ML_RG * ML_AZ)
    main = np.kron(np.eye(2), pair)
    rim = np.zeros((2, 4 * lanes, lanes))
    for parity in range(2):
        for part in range(2):
            low = parity * 4 * HALF + part * 2 * HALF
            source = part * lanes
            rim[parity, source : source + lanes, low : low + HALF] = pair[:, looks - HALF :]
            source += 2 * lanes
            rim[parity, source : source + lanes, low + HALF : low + 2 * HALF] = pair[:, :HALF]
    twiddle = twiddle.reshape(2 * shards, lanes)
    high = twiddle.astype(ml_dtypes.bfloat16).astype(np.float32)
    middle = (twiddle - high).astype(ml_dtypes.bfloat16).astype(np.float32)
    pieces = np.concatenate([high, middle, twiddle - high - middle])
    return {
        "twiddle": pieces, "forward": forward, "backward": backward, "gate_sum": gate_sum, "main": main, "rim": rim,
    }


def filtered_looks(raw_echo, range_filter, azimuth_phase, pair_offset, shards):
    dates, _, lanes, total_gates = raw_echo.shape
    gates = azimuth_phase.shape[0]
    part_gates = chunk_gates(gates)
    chunks, pairs = gates // part_gates, dates // 2
    gate_rows, looks = total_gates // ML_RG, lanes // ML_AZ
    tables = focus_tables(shards, part_gates, lanes)
    tables.update(filter_tables(gate_rows, looks, dates))
    places, pack = packed(tables)
    rows = shards * part_gates
    block = (chunks, shards, 6 * (part_gates // ML_RG), lanes)
    columns = (chunks, pairs, shards, 4 * part_gates, lanes)
    return pl.pallas_call(
        functools.partial(stack_kernel, shards, places),
        in_specs=[pl.BlockSpec(memory_space=pl.ANY)] * 5,
        out_specs=VMEM,
        out_shape=jax.ShapeDtypeStruct((dates, 2, looks, gate_rows), jnp.float32),
        scratch_shapes=[
            pltpu.VMEM(pack.shape, pack.dtype),
            pltpu.VMEM(raw_echo.shape, raw_echo.dtype),
            pltpu.VMEM(range_filter.shape, range_filter.dtype),
            pltpu.VMEM(azimuth_phase.shape, azimuth_phase.dtype),
            pltpu.VMEM(columns, jnp.bfloat16),
            pltpu.VMEM(columns, jnp.bfloat16),
            pltpu.VMEM(azimuth_phase.shape[::-1], jnp.float32),
            pltpu.VMEM((chunks, 2, rows, lanes), jnp.float32),
            pltpu.VMEM((2 * shards, lanes), jnp.float32),
            pltpu.VMEM((2 * rows, 2 * lanes), jnp.float32),
            pltpu.VMEM((dates, rows, 2 * lanes), jnp.float32),
            pltpu.VMEM(block, jnp.bfloat16),
            pltpu.VMEM(block, jnp.bfloat16),
            pltpu.VMEM((dates, gate_rows, 2 * looks), jnp.float32),
            pltpu.VMEM((pairs, gate_rows, 2 * looks), jnp.float32),
            pltpu.SMEM(pair_offset.shape, pair_offset.dtype),
            pltpu.SemaphoreType.DMA((chunks * (pairs + 1),)),
            pltpu.SemaphoreType.DMA((chunks * (pairs + 1),)),
            pltpu.SemaphoreType.DMA((5,)),
            pltpu.SemaphoreType.REGULAR((3,)),
        ],
        compiler_params=pltpu.CompilerParams(collective_id=0, has_side_effects=True, vmem_limit_bytes=54784 * 1024),
        name="stack",
    )(pair_offset, raw_echo, range_filter, azimuth_phase, pack)


def tri_window():
    return 1.0 - np.abs(np.arange(PATCH) - (PATCH - 1) / 2.0) / HALF


def patch_maps(cells, starts):
    count = len(starts)
    forward = np.zeros((cells, count, PATCH), np.complex128)
    backward = np.zeros((count, PATCH, cells), np.complex128)
    window, k = tri_window(), np.arange(PATCH)
    for patch, start in enumerate(starts):
        for a in range(PATCH):
            cell = start + a
            if 0 <= cell < cells:
                wave = np.exp(2j * np.pi / PATCH * (k * a % PATCH))
                forward[cell, patch] = np.conj(wave)
                backward[patch, :, cell] = wave * window[a] / PATCH
    return forward.reshape(cells, -1), backward.reshape(-1, cells)


def filter_tables(gate_rows, looks, dates):
    gate_starts = range(-HALF, gate_rows - HALF + 1, HALF)
    line_starts = range(0, looks + 1, HALF)
    gate_fwd, gate_back = patch_maps(gate_rows, gate_starts)
    line_fwd, _ = patch_maps(looks + PATCH, line_starts)
    _, line_back = patch_maps(looks, [start - HALF for start in line_starts])
    width = (len(line_starts) - 1) * PATCH
    span = 2 * looks

    def entry(columns, main, low, table):
        block = right_block(columns).reshape(2, looks + PATCH, -1)
        for part in range(2):
            table[main + part * looks : main + (part + 1) * looks] += block[part, HALF : HALF + looks]
            at = low + part * 2 * HALF
            table[at : at + HALF] += block[part, :HALF]
            table[at + HALF : at + 2 * HALF] += block[part, HALF + looks :]

    enter = np.zeros((2, 2 * span, 2 * width))
    for parity in range(2):
        entry(line_fwd[:, :width], 0, span + parity * 4 * HALF, enter[parity])
    wide = dates * PATCH
    extra = np.zeros((dates * span + dates // 2 * span, 2 * wide))
    back = np.zeros((dates, 2 * looks, 2 * width + 2 * wide))
    for date in range(dates):
        placed = np.zeros((looks + PATCH, wide), np.complex128)
        placed[:, date * PATCH : (date + 1) * PATCH] = line_fwd[:, width:]
        entry(placed, date * span, dates * span + date // 2 * span + date % 2 * 4 * HALF, extra)
        placed = np.zeros((wide, looks), np.complex128)
        placed[date * PATCH : (date + 1) * PATCH] = line_back[width:]
        back[date, :, : 2 * width] = right_block(line_back[:width]).T
        back[date, :, 2 * width :] = right_block(placed).T
    gap = (np.arange(PATCH)[:, None] - np.arange(PATCH)[None, :]) % PATCH
    near = (gap <= 1) | (gap == PATCH - 1)
    group = max(2 * width, wide) // PATCH
    near_line = np.kron(np.eye(group), near)
    level = np.kron(np.eye(group), np.ones((PATCH, PATCH)) / PATCH**2)
    return {
        "enter": enter,
        "extra": extra,
        "gate_fwd": left_block(gate_fwd.T),
        "near_line": near_line,
        "level": level,
        "gate_back": left_block(gate_back.T),
        "line_back": back,
    }


def packed(tables):
    places, panels, first = {}, [], 0
    for name, table in tables.items():
        stack = table.reshape((-1,) + table.shape[-2:])
        _, height, width = stack.shape
        count = -(-width // LANES)
        places[name] = (first, height, count, width)
        for part in np.pad(stack, ((0, 0), (0, 0), (0, count * LANES - width))):
            for i in range(count):
                panels.append(part[:, i * LANES : (i + 1) * LANES])
                first += height
    return places, np.concatenate(panels).astype(ml_dtypes.bfloat16)


def body(raw_echo, range_filter, azimuth_phase, pair_offset):
    shards = lax.axis_size("lines")
    image = filtered_looks(raw_echo, range_filter, azimuth_phase, pair_offset, shards)
    return image.transpose(0, 1, 3, 2)


def solution(mesh):
    placed = (P("groups", None, "lines", None), P(), P("lines", None), P())
    return jax.shard_map(
        body,
        mesh=mesh,
        in_specs=placed,
        out_specs=P("groups", None, None, "lines"),
        check_vma=False,
    )
```

```python
import functools

import jax
import jax.numpy as jnp
import ml_dtypes
import numpy as np
from jax import lax
from jax.experimental import pallas as pl
from jax.experimental.pallas import tpu as pltpu
from jax.sharding import PartitionSpec as P

ML_RG = 4
ML_AZ = 2
PATCH = 32
HALF = PATCH // 2
BOX_FLOOR = 0.25
LANES = 128
VMEM = pl.BlockSpec(memory_space=pltpu.VMEM)


def right_block(table):
    return np.block([[table.real, table.imag], [-table.imag, table.real]])


def left_block(table):
    return np.block([[table.real, -table.imag], [table.imag, table.real]])


def split(value):
    high = value.astype(jnp.bfloat16)
    low = (value - high.astype(jnp.float32)).astype(jnp.bfloat16)
    return high, low


def mm(a, b):
    return jnp.dot(a, b, preferred_element_type=jnp.float32)


def exact_times(value, table):
    high, low = split(value)
    return mm(high, table) + mm(low, table)


def fft_leading(re, im, sign):
    count = len(re)
    if count == 1:
        return re, im
    if count == 2:
        return [re[0] + re[1], re[0] - re[1]], [im[0] + im[1], im[0] - im[1]]
    er, ei = fft_leading(re[0::2], im[0::2], sign)
    odr, odi = fft_leading(re[1::2], im[1::2], sign)
    half = count // 2
    out_r, out_i = [None] * count, [None] * count
    for k in range(half):
        angle = sign * 2.0 * np.pi * k / count
        c, s = float(np.cos(angle)), float(np.sin(angle))
        if k == 0:
            tr, ti = odr[k], odi[k]
        elif 4 * k == count:
            tr, ti = (-odi[k], odr[k]) if sign > 0 else (odi[k], -odr[k])
        else:
            tr = odr[k] * c - odi[k] * s
            ti = odr[k] * s + odi[k] * c
        out_r[k], out_i[k] = er[k] + tr, ei[k] + ti
        out_r[k + half], out_i[k + half] = er[k] - tr, ei[k] - ti
    return out_r, out_i


def weigh(spectra, table):
    rows, width = spectra.shape[0] // 2, spectra.shape[1]
    re, im = spectra[:rows], spectra[rows:]
    power = (re * re + im * im).astype(jnp.bfloat16)
    shape = (rows // PATCH, PATCH, width)
    near = mm(power, table("near_line")[:width, :width]).reshape(shape)
    level = jnp.sum(mm(power, table("level")[:width, :width]).reshape(shape), axis=1)
    scale = 1.0 / (9.0 * (level + 1e-06))
    weights = []
    for patch in range(rows // PATCH):
        value = near[patch]
        value = value + pltpu.roll(value, 1, 0) + pltpu.roll(value, PATCH - 1, 0)
        value = value * scale[patch : patch + 1] + BOX_FLOOR
        weights.append(value * lax.rsqrt(value))
    weight = jnp.concatenate(weights, axis=0)
    return jnp.concatenate([re * weight, im * weight], axis=0).astype(jnp.bfloat16)


def enter_lines(cells_ref, rims_ref, table, rows):
    dates, pairs = cells_ref.shape[0], rims_ref.shape[0]
    main = [cells_ref[date, rows, :].astype(jnp.bfloat16) for date in range(dates)]
    rims = [rims_ref[pair, rows, :].astype(jnp.bfloat16) for pair in range(pairs)]
    halves = []
    for date in range(dates):
        halves.append(mm(jnp.concatenate([main[date], rims[date // 2]], axis=1), table("enter", date % 2)))
    halves.append(mm(jnp.concatenate(main + rims, axis=1), table("extra")))
    return [half.astype(jnp.bfloat16) for half in halves]


def filter_dates(entered, table, out_ref):
    dates, _, looks, gate_rows = out_ref.shape
    real, imag = [], []
    for parts in zip(*entered):
        half = parts[0] if len(parts) == 1 else jnp.concatenate(parts, axis=0)
        width = half.shape[1] // 2
        real.append(half[:, :width])
        imag.append(half[:, width:])
    groups = [(first, min(first + 2, dates + 1)) for first in range(0, dates + 1, 2)]
    spectra = []
    for first, last in groups:
        re, im = jnp.concatenate(real[first:last], axis=1), jnp.concatenate(imag[first:last], axis=1)
        spectra.append(mm(table("gate_fwd"), jnp.concatenate([re, im], axis=0)))
    weighted = [weigh(value, table) for value in spectra]
    image_re, image_im = [], []
    for (first, last), value in zip(groups, weighted):
        image = mm(table("gate_back"), value).astype(jnp.bfloat16)
        step = image.shape[1] // (last - first)
        for start in range(0, image.shape[1], step):
            image_re.append(image[:gate_rows, start : start + step])
            image_im.append(image[gate_rows:, start : start + step])
    contract = (((1,), (1,)), ((), ()))
    for date in range(dates):
        image = jnp.concatenate([image_re[date], image_im[date], image_re[dates], image_im[dates]], axis=1)
        result = lax.dot_general(table("line_back", date), image, contract, preferred_element_type=jnp.float32)
        out_ref[date, 0] = result[:looks]
        out_ref[date, 1] = result[looks:]


def chunk_gates(gates):
    return gates // 2 if gates % (2 * 4 * ML_RG) == 0 else gates


def stack_kernel(
    shards, places, offset_hbm, raw_hbm, filt_hbm, phase_hbm, pack_hbm, out_ref, pack, raw_ref, filt_ref, phase_ref,
    sent, columns, turned, trig, twid_ref, work, focused, looks_sent, looks_got, cells, rims, offset_ref, send_sem, recv_sem, load_sem, relay_sem,
):
    def table(name, index=0):
        first, height, panels, width = places[name]
        first += index * height * panels
        parts = [pack[first + i * height : first + (i + 1) * height, :] for i in range(panels)]
        whole = parts[0] if panels == 1 else jnp.concatenate(parts, axis=1)
        return whole[:, :width]

    dates, _, line_count, total_gates = raw_ref.shape
    chunks, pairs, _, block_rows, lanes = columns.shape
    gates = total_gates // shards
    part_gates = gates // chunks
    me = lax.axis_index("lines")

    loads = [
        pltpu.make_async_copy(source, target, load_sem.at[i])
        for i, (source, target) in enumerate(
            [(filt_hbm, filt_ref), (raw_hbm, raw_ref), (phase_hbm, phase_ref), (pack_hbm, pack), (offset_hbm, offset_ref)]
        )
    ]
    loads[0].start()
    loads[1].start()

    def ring(step):
        return lax.rem(me + step, shards)

    barrier = pltpu.get_barrier_semaphore()

    def signal(sem, peer):
        pl.semaphore_signal(sem, inc=1, device_id={"lines": peer}, device_id_type=pl.DeviceIdType.MESH)

    quarter = shards // 4
    mine = me // quarter
    @pl.loop(1, shards)
    def _(step):
        peer = ring(step)

        @pl.when(peer // quarter >= mine - 1)
        def _():
            signal(barrier, peer)


    def compress(chunk, pair):
        weights = filt_ref[...]
        if chunks > 1:
            weights = weights.reshape(2, shards, chunks, part_gates, total_gates)[:, :, chunk]
        weights = weights.reshape(2 * shards * part_gates, total_gates)
        half = shards * part_gates
        contract = (((1,), (1,)), ((), ()))
        for i in range(2):
            lines = raw_ref[2 * pair + i].reshape(2 * line_count, total_gates)
            product = lax.dot_general(weights, lines, contract, preferred_element_type=jnp.float32)
            real = product[:half, :line_count] - product[half:, line_count:]
            imag = product[half:, :line_count] + product[:half, line_count:]
            shape = (shards, part_gates, line_count)
            both = jnp.concatenate([real.reshape(shape), imag.reshape(shape)], axis=1)
            at = pl.ds(2 * i * part_gates, 2 * part_gates)
            sent[chunk, pair, :, at, :] = both.astype(jnp.bfloat16)

    def block(source, target, slot, peer):
        return pltpu.make_async_remote_copy(
            src_ref=source, dst_ref=target, send_sem=send_sem.at[slot], recv_sem=recv_sem.at[slot],
            device_id={"lines": peer}, device_id_type=pl.DeviceIdType.MESH,
        )

    def send_block(chunk, pair, peer):
        block(sent.at[chunk, pair, peer], columns.at[chunk, pair, me], chunk * pairs + pair, peer).start()

    def send_part(chunk, pair):
        @pl.loop(1, shards)
        def _(step):
            send_block(chunk, pair, ring(step))

        columns[chunk, pair, me] = sent[chunk, pair, me]

    def send_looks(chunk):
        @pl.loop(1, shards)
        def _(step):
            peer = ring(step)
            block(looks_sent.at[chunk, peer], looks_got.at[chunk, me], chunks * pairs + chunk, peer).start()

        looks_got[chunk, me] = looks_sent[chunk, me]

    def arrived(chunk, pair):
        part = pl.ds(0, shards - 1)
        slot = chunk * pairs + pair
        return block(sent.at[chunk, pair, part], columns.at[chunk, pair, part], slot, ring(1))

    def gathered(chunk):
        part = pl.ds(0, shards - 1)
        return block(looks_sent.at[chunk, part], looks_got.at[chunk, part], chunks * pairs + chunk, ring(1))

    loads[0].wait()
    loads[1].wait()
    for load in loads[2:]:
        load.start()
    for chunk in range(chunks):
        if chunk == 0:
            compress(0, 0)
            pl.semaphore_wait(barrier, jnp.minimum(mine + 2, 4) * quarter - 1)

            @pl.when((mine == 1) | (mine == 2))
            def _():
                signal(relay_sem.at[0], me - quarter)

            @pl.loop(1, shards)
            def _(step):
                peer = ring(step)

                @pl.when(peer // quarter <= mine + 1)
                def _():
                    send_block(0, 0, peer)

            @pl.when(mine < 2)
            def _():
                pl.semaphore_wait(relay_sem.at[0], 1)

                @pl.when(mine == 1)
                def _():
                    signal(relay_sem.at[1], me - quarter)

                @pl.loop(0, quarter)
                def _(step):
                    send_block(0, 0, (mine + 2) * quarter + step)

            @pl.loop(1, pairs)
            def _(pair):
                compress(0, pair)

            @pl.when(mine == 0)
            def _():
                pl.semaphore_wait(relay_sem.at[1], 1)

                @pl.loop(0, quarter)
                def _(step):
                    send_block(0, 0, 3 * quarter + step)

            columns[0, 0, me] = sent[0, 0, me]

            @pl.loop(1, pairs)
            def _(pair):
                send_part(0, pair)
        else:
            @pl.loop(0, pairs)
            def _(pair):
                compress(chunk, pair)
                send_part(chunk, pair)

    loads[2].wait()
    turned[...] = phase_ref[...].T

    @pl.loop(0, shards)
    def _(k):
        phase = turned[pl.ds(k, lanes, stride=shards), :].T
        at = pl.ds(pl.multiple_of(k * part_gates, part_gates), part_gates)
        cosine, sine = jnp.cos(phase), jnp.sin(phase)
        for chunk in range(chunks):
            trig[chunk, 0, at, :] = cosine[chunk * part_gates : (chunk + 1) * part_gates]
            trig[chunk, 1, at, :] = sine[chunk * part_gates : (chunk + 1) * part_gates]

    loads[3].wait()
    loads[4].wait()
    pieces = table("twiddle").astype(jnp.float32)
    count = twid_ref.shape[0]
    twid_ref[...] = pieces[:count] + pieces[count : 2 * count] + pieces[2 * count :]
    rows = shards * part_gates
    looks_rows = places["gate_sum"][1] // 3
    tile = looks_rows // shards

    @pl.loop(0, chunks)
    def _(chunk):
        @pl.loop(0, pairs)
        def _(pair):
            arrived(chunk, pair).wait_recv()

            @pl.when((chunk > 0) & (pair == pairs - 1))
            def _():
                send_looks(chunk - 1)

            for i in range(2):
                start = 2 * i * part_gates
                data = [
                    columns[chunk, pair, s, pl.ds(start, 2 * part_gates), :].astype(jnp.float32) for s in range(shards)
                ]
                for low in range(0, part_gates, 8):
                    re = [value[low : low + 8] for value in data]
                    im = [value[part_gates + low : part_gates + low + 8] for value in data]
                    re, im = fft_leading(re, im, -1.0)
                    for k in range(shards):
                        c, s = twid_ref[pl.ds(k, 1), :], twid_ref[pl.ds(shards + k, 1), :]
                        at = pl.ds(i * rows + k * part_gates + low, 8)
                        work[at, :lanes] = re[k] * c + im[k] * s
                        work[at, lanes:] = im[k] * c - re[k] * s
            spectrum = mm(work[...].astype(jnp.bfloat16), table("forward"))
            c, s = trig[chunk, 0], trig[chunk, 1]
            shifted = []
            for i in range(2):
                re, im = spectrum[i * rows : (i + 1) * rows, :lanes], spectrum[i * rows : (i + 1) * rows, lanes:]
                shifted.append(jnp.concatenate([re * c - im * s, re * s + im * c], axis=1))
            work[...] = mm(jnp.concatenate(shifted, axis=0).astype(jnp.bfloat16), table("backward"))
            for i in range(2):
                for low in range(0, part_gates, 8):
                    re, im = [], []
                    for k in range(shards):
                        c, s = twid_ref[pl.ds(k, 1), :], twid_ref[pl.ds(shards + k, 1), :]
                        at = pl.ds(i * rows + k * part_gates + low, 8)
                        a, b = work[at, :lanes], work[at, lanes:]
                        re.append(a * c - b * s)
                        im.append(b * c + a * s)
                    re, im = fft_leading(re, im, 1.0)
                    for n in range(shards):
                        at = pl.ds(n * part_gates + low, 8)
                        focused[2 * pair + i, at, :lanes] = re[n].astype(jnp.bfloat16).astype(jnp.float32)
                        focused[2 * pair + i, at, lanes:] = im[n].astype(jnp.bfloat16).astype(jnp.float32)

        joined = []
        for parity in range(2):
            parts = []
            for d in (parity, parity + 2):
                partner = lax.rem(d + offset_ref[d], dates)
                a, b = focused[d, :, :lanes], focused[d, :, lanes:]
                p, q = focused[partner, :, :lanes], focused[partner, :, lanes:]
                parts.append(jnp.concatenate([a * p + b * q, b * p - a * q], axis=1).astype(jnp.bfloat16))
            joined.append(jnp.concatenate(parts, axis=0))
        summed = [mm(table("gate_sum"), value).astype(jnp.bfloat16) for value in joined]
        pieces = [mm(value[:looks_rows], table("main")) for value in summed]
        sides = [jnp.concatenate([value[looks_rows : 2 * looks_rows], value[2 * looks_rows :]], axis=1) for value in summed]
        rim = mm(sides[0], table("rim", 0)) + mm(sides[1], table("rim", 1))
        shaped = [piece.reshape(shards, tile, lanes) for piece in pieces + [rim]]
        looks_sent[chunk] = jnp.concatenate(shaped, axis=1).astype(looks_sent.dtype)

        @pl.when(chunk == chunks - 1)
        def _():
            send_looks(chunk)

    @pl.loop(0, chunks)
    def _(chunk):
        @pl.loop(0, pairs)
        def _(pair):
            arrived(chunk, pair).wait_send()

    part_looks = tile // 2
    entered = []
    for chunk in range(chunks):
        gathered(chunk).wait_recv()
        for shard in range(shards):
            received = looks_got[chunk, shard].astype(jnp.float32)
            at = pl.ds((chunk * shards + shard) * part_looks, part_looks)
            for q in range(2):
                for parity in range(2):
                    low = parity * tile + q * part_looks
                    cells[2 * q + parity, at, :] = received[low : low + part_looks]
                low = 2 * tile + q * part_looks
                rims[q, at, :] = received[low : low + part_looks]

        height = shards * part_looks
        entered.append(enter_lines(cells, rims, table, slice(chunk * height, (chunk + 1) * height)))

    filter_dates(entered, table, out_ref)

    @pl.loop(0, chunks)
    def _(chunk):
        gathered(chunk).wait_send()


def focus_tables(shards, part_gates, lanes):
    total = shards * lanes
    k1, n2 = np.arange(shards), np.arange(lanes)
    angle = 2.0 * np.pi / total * (np.outer(k1, n2) % total)
    twiddle = np.stack([np.cos(angle), np.sin(angle)]).astype(np.float32)
    grid = np.exp(-2j * np.pi / lanes * (np.outer(n2, n2) % lanes))
    forward = right_block(grid)
    backward = right_block(np.conj(grid)) / total
    group = np.kron(np.eye(part_gates // ML_RG), np.ones((1, ML_RG)))
    gate_sum = []
    for shift in (0, -1, 1):
        spread = np.einsum("js,qr,lg->jqlrsg", np.eye(shards, k=shift), np.eye(2), group)
        gate_sum.append(spread.reshape(shards * 2 * group.shape[0], -1))
    gate_sum = np.concatenate(gate_sum)
    looks = lanes // ML_AZ
    pair = np.kron(np.eye(looks), np.ones((ML_AZ, 1))) / (ML_RG * ML_AZ)
    main = np.kron(np.eye(2), pair)
    rim = np.zeros((2, 4 * lanes, lanes))
    for parity in range(2):
        for part in range(2):
            low = parity * 4 * HALF + part * 2 * HALF
            source = part * lanes
            rim[parity, source : source + lanes, low : low + HALF] = pair[:, looks - HALF :]
            source += 2 * lanes
            rim[parity, source : source + lanes, low + HALF : low + 2 * HALF] = pair[:, :HALF]
    twiddle = twiddle.reshape(2 * shards, lanes)
    high = twiddle.astype(ml_dtypes.bfloat16).astype(np.float32)
    middle = (twiddle - high).astype(ml_dtypes.bfloat16).astype(np.float32)
    pieces = np.concatenate([high, middle, twiddle - high - middle])
    return {
        "twiddle": pieces, "forward": forward, "backward": backward, "gate_sum": gate_sum, "main": main, "rim": rim,
    }


def filtered_looks(raw_echo, range_filter, azimuth_phase, pair_offset, shards):
    dates, _, lanes, total_gates = raw_echo.shape
    gates = azimuth_phase.shape[0]
    part_gates = chunk_gates(gates)
    chunks, pairs = gates // part_gates, dates // 2
    gate_rows, looks = total_gates // ML_RG, lanes // ML_AZ
    tables = focus_tables(shards, part_gates, lanes)
    order = np.arange(gate_rows).reshape(shards, chunks, -1).transpose(1, 0, 2).ravel()
    tables.update(filter_tables(order, looks, dates))
    places, pack = packed(tables)
    rows = shards * part_gates
    block = (chunks, shards, 6 * (part_gates // ML_RG), lanes)
    columns = (chunks, pairs, shards, 4 * part_gates, lanes)
    return pl.pallas_call(
        functools.partial(stack_kernel, shards, places),
        in_specs=[pl.BlockSpec(memory_space=pl.ANY)] * 5,
        out_specs=VMEM,
        out_shape=jax.ShapeDtypeStruct((dates, 2, looks, gate_rows), jnp.float32),
        scratch_shapes=[
            pltpu.VMEM(pack.shape, pack.dtype),
            pltpu.VMEM(raw_echo.shape, raw_echo.dtype),
            pltpu.VMEM(range_filter.shape, range_filter.dtype),
            pltpu.VMEM(azimuth_phase.shape, azimuth_phase.dtype),
            pltpu.VMEM(columns, jnp.bfloat16),
            pltpu.VMEM(columns, jnp.bfloat16),
            pltpu.VMEM(azimuth_phase.shape[::-1], jnp.float32),
            pltpu.VMEM((chunks, 2, rows, lanes), jnp.float32),
            pltpu.VMEM((2 * shards, lanes), jnp.float32),
            pltpu.VMEM((2 * rows, 2 * lanes), jnp.float32),
            pltpu.VMEM((dates, rows, 2 * lanes), jnp.float32),
            pltpu.VMEM(block, jnp.bfloat16),
            pltpu.VMEM(block, jnp.bfloat16),
            pltpu.VMEM((dates, gate_rows, 2 * looks), jnp.float32),
            pltpu.VMEM((pairs, gate_rows, 2 * looks), jnp.float32),
            pltpu.SMEM(pair_offset.shape, pair_offset.dtype),
            pltpu.SemaphoreType.DMA((chunks * (pairs + 1),)),
            pltpu.SemaphoreType.DMA((chunks * (pairs + 1),)),
            pltpu.SemaphoreType.DMA((5,)),
            pltpu.SemaphoreType.REGULAR((2,)),
        ],
        compiler_params=pltpu.CompilerParams(collective_id=0, has_side_effects=True, vmem_limit_bytes=54784 * 1024),
        name="stack",
    )(pair_offset, raw_echo, range_filter, azimuth_phase, pack)


def tri_window():
    return 1.0 - np.abs(np.arange(PATCH) - (PATCH - 1) / 2.0) / HALF


def patch_maps(cells, starts):
    count = len(starts)
    forward = np.zeros((cells, count, PATCH), np.complex128)
    backward = np.zeros((count, PATCH, cells), np.complex128)
    window, k = tri_window(), np.arange(PATCH)
    for patch, start in enumerate(starts):
        for a in range(PATCH):
            cell = start + a
            if 0 <= cell < cells:
                wave = np.exp(2j * np.pi / PATCH * (k * a % PATCH))
                forward[cell, patch] = np.conj(wave)
                backward[patch, :, cell] = wave * window[a] / PATCH
    return forward.reshape(cells, -1), backward.reshape(-1, cells)


def filter_tables(order, looks, dates):
    gate_rows = order.size
    gate_starts = range(-HALF, gate_rows - HALF + 1, HALF)
    line_starts = range(0, looks + 1, HALF)
    gate_fwd, gate_back = patch_maps(gate_rows, gate_starts)
    line_fwd, _ = patch_maps(looks + PATCH, line_starts)
    _, line_back = patch_maps(looks, [start - HALF for start in line_starts])
    width = (len(line_starts) - 1) * PATCH
    span = 2 * looks

    def entry(columns, main, low, table):
        block = right_block(columns).reshape(2, looks + PATCH, -1)
        for part in range(2):
            table[main + part * looks : main + (part + 1) * looks] += block[part, HALF : HALF + looks]
            at = low + part * 2 * HALF
            table[at : at + HALF] += block[part, :HALF]
            table[at + HALF : at + 2 * HALF] += block[part, HALF + looks :]

    enter = np.zeros((2, 2 * span, 2 * width))
    for parity in range(2):
        entry(line_fwd[:, :width], 0, span + parity * 4 * HALF, enter[parity])
    wide = dates * PATCH
    extra = np.zeros((dates * span + dates // 2 * span, 2 * wide))
    back = np.zeros((dates, 2 * looks, 2 * width + 2 * wide))
    for date in range(dates):
        placed = np.zeros((looks + PATCH, wide), np.complex128)
        placed[:, date * PATCH : (date + 1) * PATCH] = line_fwd[:, width:]
        entry(placed, date * span, dates * span + date // 2 * span + date % 2 * 4 * HALF, extra)
        placed = np.zeros((wide, looks), np.complex128)
        placed[date * PATCH : (date + 1) * PATCH] = line_back[width:]
        back[date, :, : 2 * width] = right_block(line_back[:width]).T
        back[date, :, 2 * width :] = right_block(placed).T
    gap = (np.arange(PATCH)[:, None] - np.arange(PATCH)[None, :]) % PATCH
    near = (gap <= 1) | (gap == PATCH - 1)
    group = max(2 * width, wide) // PATCH
    near_line = np.kron(np.eye(group), near)
    level = np.kron(np.eye(group), np.ones((PATCH, PATCH)) / PATCH**2)
    return {
        "enter": enter,
        "extra": extra,
        "gate_fwd": left_block(gate_fwd[order].T),
        "near_line": near_line,
        "level": level,
        "gate_back": left_block(gate_back.T),
        "line_back": back,
    }


def packed(tables):
    places, panels, first = {}, [], 0
    for name, table in tables.items():
        stack = table.reshape((-1,) + table.shape[-2:])
        _, height, width = stack.shape
        count = -(-width // LANES)
        places[name] = (first, height, count, width)
        for part in np.pad(stack, ((0, 0), (0, 0), (0, count * LANES - width))):
            for i in range(count):
                panels.append(part[:, i * LANES : (i + 1) * LANES])
                first += height
    return places, np.concatenate(panels).astype(ml_dtypes.bfloat16)


def body(raw_echo, range_filter, azimuth_phase, pair_offset):
    shards = lax.axis_size("lines")
    image = filtered_looks(raw_echo, range_filter, azimuth_phase, pair_offset, shards)
    return image.transpose(0, 1, 3, 2)


def solution(mesh):
    placed = (P("groups", None, "lines", None), P(), P("lines", None), P())
    return jax.shard_map(
        body,
        mesh=mesh,
        in_specs=placed,
        out_specs=P("groups", None, None, "lines"),
        check_vma=False,
    )
```

```python
import functools

import jax
import jax.numpy as jnp
import ml_dtypes
import numpy as np
from jax import lax
from jax.experimental import pallas as pl
from jax.experimental.pallas import tpu as pltpu
from jax.sharding import PartitionSpec as P

ML_RG = 4
ML_AZ = 2
PATCH = 32
HALF = PATCH // 2
BOX_FLOOR = 0.25
LANES = 128
VMEM = pl.BlockSpec(memory_space=pltpu.VMEM)


def right_block(table):
    return np.block([[table.real, table.imag], [-table.imag, table.real]])


def left_block(table):
    return np.block([[table.real, -table.imag], [table.imag, table.real]])


def split(value):
    high = value.astype(jnp.bfloat16)
    low = (value - high.astype(jnp.float32)).astype(jnp.bfloat16)
    return high, low


def mm(a, b):
    return jnp.dot(a, b, preferred_element_type=jnp.float32)


def exact_times(value, table):
    high, low = split(value)
    return mm(high, table) + mm(low, table)


def fft_leading(re, im, sign):
    count = len(re)
    if count == 1:
        return re, im
    if count == 2:
        return [re[0] + re[1], re[0] - re[1]], [im[0] + im[1], im[0] - im[1]]
    er, ei = fft_leading(re[0::2], im[0::2], sign)
    odr, odi = fft_leading(re[1::2], im[1::2], sign)
    half = count // 2
    out_r, out_i = [None] * count, [None] * count
    for k in range(half):
        angle = sign * 2.0 * np.pi * k / count
        c, s = float(np.cos(angle)), float(np.sin(angle))
        if k == 0:
            tr, ti = odr[k], odi[k]
        elif 4 * k == count:
            tr, ti = (-odi[k], odr[k]) if sign > 0 else (odi[k], -odr[k])
        else:
            tr = odr[k] * c - odi[k] * s
            ti = odr[k] * s + odi[k] * c
        out_r[k], out_i[k] = er[k] + tr, ei[k] + ti
        out_r[k + half], out_i[k + half] = er[k] - tr, ei[k] - ti
    return out_r, out_i


def weigh(spectra, table):
    rows, width = spectra.shape[0] // 2, spectra.shape[1]
    re, im = spectra[:rows], spectra[rows:]
    power = (re * re + im * im).astype(jnp.bfloat16)
    shape = (rows // PATCH, PATCH, width)
    near = mm(power, table("near_line")[:width, :width]).reshape(shape)
    level = jnp.sum(mm(power, table("level")[:width, :width]).reshape(shape), axis=1)
    scale = 1.0 / (9.0 * (level + 1e-06))
    weights = []
    for patch in range(rows // PATCH):
        value = near[patch]
        value = value + pltpu.roll(value, 1, 0) + pltpu.roll(value, PATCH - 1, 0)
        value = value * scale[patch : patch + 1] + BOX_FLOOR
        weights.append(value * lax.rsqrt(value))
    weight = jnp.concatenate(weights, axis=0)
    return jnp.concatenate([re * weight, im * weight], axis=0).astype(jnp.bfloat16)


def filter_dates(cells_ref, rims_ref, table, out_ref):
    dates, _, looks, gate_rows = out_ref.shape
    main = [cells_ref[date].astype(jnp.bfloat16) for date in range(dates)]
    rims = [rims_ref[pair].astype(jnp.bfloat16) for pair in range(dates // 2)]
    real, imag = [], []
    for date in range(dates):
        half = mm(jnp.concatenate([main[date], rims[date // 2]], axis=1), table("enter", date % 2)).astype(jnp.bfloat16)
        width = half.shape[1] // 2
        real.append(half[:, :width])
        imag.append(half[:, width:])
    half = mm(jnp.concatenate(main + rims, axis=1), table("extra")).astype(jnp.bfloat16)
    width = half.shape[1] // 2
    real.append(half[:, :width])
    imag.append(half[:, width:])
    groups = [(first, min(first + 2, dates + 1)) for first in range(0, dates + 1, 2)]
    spectra = []
    for first, last in groups:
        re, im = jnp.concatenate(real[first:last], axis=1), jnp.concatenate(imag[first:last], axis=1)
        spectra.append(mm(table("gate_fwd"), jnp.concatenate([re, im], axis=0)))
    weighted = [weigh(value, table) for value in spectra]
    image_re, image_im = [], []
    for (first, last), value in zip(groups, weighted):
        image = mm(table("gate_back"), value).astype(jnp.bfloat16)
        step = image.shape[1] // (last - first)
        for start in range(0, image.shape[1], step):
            image_re.append(image[:gate_rows, start : start + step])
            image_im.append(image[gate_rows:, start : start + step])
    contract = (((1,), (1,)), ((), ()))
    for date in range(dates):
        image = jnp.concatenate([image_re[date], image_im[date], image_re[dates], image_im[dates]], axis=1)
        result = lax.dot_general(table("line_back", date), image, contract, preferred_element_type=jnp.float32)
        out_ref[date, 0] = result[:looks]
        out_ref[date, 1] = result[looks:]


def chunk_gates(gates):
    return gates // 2 if gates % (2 * 4 * ML_RG) == 0 else gates


def stack_kernel(
    shards, places, offset_hbm, raw_hbm, filt_hbm, phase_hbm, pack_hbm, out_ref, pack, raw_ref, filt_ref, phase_ref,
    sent, columns, turned, trig, twid_ref, work, focused, looks_sent, looks_got, cells, rims, offset_ref, send_sem, recv_sem, load_sem, relay_sem,
):
    def table(name, index=0):
        first, height, panels, width = places[name]
        first += index * height * panels
        parts = [pack[first + i * height : first + (i + 1) * height, :] for i in range(panels)]
        whole = parts[0] if panels == 1 else jnp.concatenate(parts, axis=1)
        return whole[:, :width]

    dates, _, line_count, total_gates = raw_ref.shape
    chunks, pairs, _, block_rows, lanes = columns.shape
    gates = total_gates // shards
    part_gates = gates // chunks
    me = lax.axis_index("lines")

    loads = [
        pltpu.make_async_copy(source, target, load_sem.at[i])
        for i, (source, target) in enumerate(
            [(filt_hbm, filt_ref), (raw_hbm, raw_ref), (phase_hbm, phase_ref), (pack_hbm, pack), (offset_hbm, offset_ref)]
        )
    ]
    loads[0].start()
    loads[1].start()

    def ring(step):
        return lax.rem(me + step, shards)

    barrier = pltpu.get_barrier_semaphore()

    def signal(sem, peer):
        pl.semaphore_signal(sem, inc=1, device_id={"lines": peer}, device_id_type=pl.DeviceIdType.MESH)

    quarter = shards // 4
    mine = me // quarter
    outer = (mine == 0) | (mine == 3)
    opposite = lax.rem(mine + 2, 4)

    def is_near(peer):
        place = peer // quarter
        return (place != opposite) & jnp.logical_not(outer & (place == 3 - mine))

    @pl.loop(1, shards)
    def _(step):
        peer = ring(step)

        @pl.when(is_near(peer))
        def _():
            signal(barrier, peer)


    def compress(chunk, pair):
        weights = filt_ref[...]
        if chunks > 1:
            weights = weights.reshape(2, shards, chunks, part_gates, total_gates)[:, :, chunk]
        weights = weights.reshape(2 * shards * part_gates, total_gates)
        half = shards * part_gates
        contract = (((1,), (1,)), ((), ()))
        for i in range(2):
            lines = raw_ref[2 * pair + i].reshape(2 * line_count, total_gates)
            product = lax.dot_general(weights, lines, contract, preferred_element_type=jnp.float32)
            real = product[:half, :line_count] - product[half:, line_count:]
            imag = product[half:, :line_count] + product[:half, line_count:]
            shape = (shards, part_gates, line_count)
            both = jnp.concatenate([real.reshape(shape), imag.reshape(shape)], axis=1)
            at = pl.ds(2 * i * part_gates, 2 * part_gates)
            sent[chunk, pair, :, at, :] = both.astype(jnp.bfloat16)

    def block(source, target, slot, peer):
        return pltpu.make_async_remote_copy(
            src_ref=source, dst_ref=target, send_sem=send_sem.at[slot], recv_sem=recv_sem.at[slot],
            device_id={"lines": peer}, device_id_type=pl.DeviceIdType.MESH,
        )

    def send_block(chunk, pair, peer):
        block(sent.at[chunk, pair, peer], columns.at[chunk, pair, me], chunk * pairs + pair, peer).start()

    def send_whole(chunk):
        @pl.loop(1, shards)
        def _(step):
            peer = ring(step)
            block(sent.at[chunk, :, peer], columns.at[chunk, :, me], chunk * pairs, peer).start()

        columns[chunk, :, me] = sent[chunk, :, me]

    def arrived_whole(chunk):
        part = pl.ds(0, shards - 1)
        return block(sent.at[chunk, :, part], columns.at[chunk, :, part], chunk * pairs, ring(1))

    def send_part(chunk, pair):
        @pl.loop(1, shards)
        def _(step):
            send_block(chunk, pair, ring(step))

        columns[chunk, pair, me] = sent[chunk, pair, me]

    def send_looks(chunk):
        @pl.loop(1, shards)
        def _(step):
            peer = jnp.where(step > me, step, step - 1)
            block(looks_sent.at[chunk, peer], looks_got.at[chunk, me], chunks * pairs + chunk, peer).start()

        looks_got[chunk, me] = looks_sent[chunk, me]

    def arrived(chunk, pair):
        part = pl.ds(0, shards - 1)
        slot = chunk * pairs + pair
        return block(sent.at[chunk, pair, part], columns.at[chunk, pair, part], slot, ring(1))

    def gathered(chunk):
        part = pl.ds(0, shards - 1)
        return block(looks_sent.at[chunk, part], looks_got.at[chunk, part], chunks * pairs + chunk, ring(1))

    loads[0].wait()
    loads[1].wait()
    for load in loads[2:]:
        load.start()
    for chunk in range(chunks):
        if chunk == 0:
            compress(0, 0)
            pl.semaphore_wait(barrier, jnp.where(outer, 2 * quarter - 1, 3 * quarter - 1))

            @pl.when(jnp.logical_not(outer))
            def _():
                signal(relay_sem.at[0], me - quarter)
                signal(relay_sem.at[1], me + quarter)

            @pl.loop(1, shards)
            def _(step):
                peer = ring(step)

                @pl.when(is_near(peer))
                def _():
                    send_block(0, 0, peer)

            @pl.when(mine < 2)
            def _():
                pl.semaphore_wait(relay_sem.at[0], 1)

            @pl.when(mine >= 2)
            def _():
                pl.semaphore_wait(relay_sem.at[1], 1)

            @pl.when(mine == 1)
            def _():
                signal(relay_sem.at[2], me - quarter)

            @pl.when(mine == 2)
            def _():
                signal(relay_sem.at[2], me + quarter)

            @pl.loop(0, quarter)
            def _(step):
                send_block(0, 0, opposite * quarter + step)

            @pl.loop(1, pairs)
            def _(pair):
                compress(0, pair)

            @pl.when(outer)
            def _():
                pl.semaphore_wait(relay_sem.at[2], 1)

                @pl.loop(0, quarter)
                def _(step):
                    send_block(0, 0, (3 - mine) * quarter + step)

            columns[0, 0, me] = sent[0, 0, me]

            @pl.loop(1, pairs)
            def _(pair):
                send_part(0, pair)
        else:
            @pl.loop(0, pairs)
            def _(pair):
                compress(chunk, pair)

            send_whole(chunk)

    loads[2].wait()
    turned[...] = phase_ref[...].T

    @pl.loop(0, shards)
    def _(k):
        phase = turned[pl.ds(k, lanes, stride=shards), :].T
        at = pl.ds(pl.multiple_of(k * part_gates, part_gates), part_gates)
        cosine, sine = jnp.cos(phase), jnp.sin(phase)
        for chunk in range(chunks):
            trig[chunk, 0, at, :] = cosine[chunk * part_gates : (chunk + 1) * part_gates]
            trig[chunk, 1, at, :] = sine[chunk * part_gates : (chunk + 1) * part_gates]

    loads[3].wait()
    loads[4].wait()
    pieces = table("twiddle").astype(jnp.float32)
    count = twid_ref.shape[0]
    twid_ref[...] = pieces[:count] + pieces[count : 2 * count] + pieces[2 * count :]
    rows = shards * part_gates
    looks_rows = places["gate_sum"][1] // 3
    tile = looks_rows // shards

    @pl.loop(0, chunks)
    def _(chunk):
        @pl.loop(0, pairs)
        def _(pair):
            @pl.when(chunk == 0)
            def _():
                arrived(0, pair).wait_recv()

            @pl.when((chunk > 0) & (pair == 0))
            def _():
                arrived_whole(chunk).wait_recv()
                send_looks(chunk - 1)

            for i in range(2):
                start = 2 * i * part_gates
                data = [
                    columns[chunk, pair, s, pl.ds(start, 2 * part_gates), :].astype(jnp.float32) for s in range(shards)
                ]
                for low in range(0, part_gates, 8):
                    re = [value[low : low + 8] for value in data]
                    im = [value[part_gates + low : part_gates + low + 8] for value in data]
                    re, im = fft_leading(re, im, -1.0)
                    for k in range(shards):
                        c, s = twid_ref[pl.ds(k, 1), :], twid_ref[pl.ds(shards + k, 1), :]
                        at = pl.ds(i * rows + k * part_gates + low, 8)
                        work[at, :lanes] = re[k] * c + im[k] * s
                        work[at, lanes:] = im[k] * c - re[k] * s
            spectrum = mm(work[...].astype(jnp.bfloat16), table("forward"))
            c, s = trig[chunk, 0], trig[chunk, 1]
            shifted = []
            for i in range(2):
                re, im = spectrum[i * rows : (i + 1) * rows, :lanes], spectrum[i * rows : (i + 1) * rows, lanes:]
                shifted.append(jnp.concatenate([re * c - im * s, re * s + im * c], axis=1))
            work[...] = mm(jnp.concatenate(shifted, axis=0).astype(jnp.bfloat16), table("backward"))
            for i in range(2):
                for low in range(0, part_gates, 8):
                    re, im = [], []
                    for k in range(shards):
                        c, s = twid_ref[pl.ds(k, 1), :], twid_ref[pl.ds(shards + k, 1), :]
                        at = pl.ds(i * rows + k * part_gates + low, 8)
                        a, b = work[at, :lanes], work[at, lanes:]
                        re.append(a * c - b * s)
                        im.append(b * c + a * s)
                    re, im = fft_leading(re, im, 1.0)
                    for n in range(shards):
                        at = pl.ds(n * part_gates + low, 8)
                        focused[2 * pair + i, at, :lanes] = re[n].astype(jnp.bfloat16).astype(jnp.float32)
                        focused[2 * pair + i, at, lanes:] = im[n].astype(jnp.bfloat16).astype(jnp.float32)

        joined = []
        for parity in range(2):
            parts = []
            for d in (parity, parity + 2):
                partner = lax.rem(d + offset_ref[d], dates)
                a, b = focused[d, :, :lanes], focused[d, :, lanes:]
                p, q = focused[partner, :, :lanes], focused[partner, :, lanes:]
                parts.append(jnp.concatenate([a * p + b * q, b * p - a * q], axis=1).astype(jnp.bfloat16))
            joined.append(jnp.concatenate(parts, axis=0))
        summed = [mm(table("gate_sum"), value).astype(jnp.bfloat16) for value in joined]
        pieces = [mm(value[:looks_rows], table("main")) for value in summed]
        sides = [jnp.concatenate([value[looks_rows : 2 * looks_rows], value[2 * looks_rows :]], axis=1) for value in summed]
        rim = mm(sides[0], table("rim", 0)) + mm(sides[1], table("rim", 1))
        shaped = [piece.reshape(shards, tile, lanes) for piece in pieces + [rim]]
        looks_sent[chunk] = jnp.concatenate(shaped, axis=1).astype(looks_sent.dtype)

        @pl.when(chunk == chunks - 1)
        def _():
            send_looks(chunk)

    @pl.loop(0, pairs)
    def _(pair):
        arrived(0, pair).wait_send()

    @pl.loop(1, chunks)
    def _(chunk):
        arrived_whole(chunk).wait_send()

    part_looks = tile // 2
    for chunk in range(chunks):
        gathered(chunk).wait_recv()
        for shard in range(shards):
            received = looks_got[chunk, shard].astype(jnp.float32)
            at = pl.ds((shard * chunks + chunk) * part_looks, part_looks)
            for q in range(2):
                for parity in range(2):
                    low = parity * tile + q * part_looks
                    cells[2 * q + parity, at, :] = received[low : low + part_looks]
                low = 2 * tile + q * part_looks
                rims[q, at, :] = received[low : low + part_looks]

    filter_dates(cells, rims, table, out_ref)

    @pl.loop(0, chunks)
    def _(chunk):
        gathered(chunk).wait_send()


def focus_tables(shards, part_gates, lanes):
    total = shards * lanes
    k1, n2 = np.arange(shards), np.arange(lanes)
    angle = 2.0 * np.pi / total * (np.outer(k1, n2) % total)
    twiddle = np.stack([np.cos(angle), np.sin(angle)]).astype(np.float32)
    grid = np.exp(-2j * np.pi / lanes * (np.outer(n2, n2) % lanes))
    forward = right_block(grid)
    backward = right_block(np.conj(grid)) / total
    group = np.kron(np.eye(part_gates // ML_RG), np.ones((1, ML_RG)))
    gate_sum = []
    for shift in (0, -1, 1):
        spread = np.einsum("js,qr,lg->jqlrsg", np.eye(shards, k=shift), np.eye(2), group)
        gate_sum.append(spread.reshape(shards * 2 * group.shape[0], -1))
    gate_sum = np.concatenate(gate_sum)
    looks = lanes // ML_AZ
    pair = np.kron(np.eye(looks), np.ones((ML_AZ, 1))) / (ML_RG * ML_AZ)
    main = np.kron(np.eye(2), pair)
    rim = np.zeros((2, 4 * lanes, lanes))
    for parity in range(2):
        for part in range(2):
            low = parity * 4 * HALF + part * 2 * HALF
            source = part * lanes
            rim[parity, source : source + lanes, low : low + HALF] = pair[:, looks - HALF :]
            source += 2 * lanes
            rim[parity, source : source + lanes, low + HALF : low + 2 * HALF] = pair[:, :HALF]
    twiddle = twiddle.reshape(2 * shards, lanes)
    high = twiddle.astype(ml_dtypes.bfloat16).astype(np.float32)
    middle = (twiddle - high).astype(ml_dtypes.bfloat16).astype(np.float32)
    pieces = np.concatenate([high, middle, twiddle - high - middle])
    return {
        "twiddle": pieces, "forward": forward, "backward": backward, "gate_sum": gate_sum, "main": main, "rim": rim,
    }


def filtered_looks(raw_echo, range_filter, azimuth_phase, pair_offset, shards):
    dates, _, lanes, total_gates = raw_echo.shape
    gates = azimuth_phase.shape[0]
    part_gates = chunk_gates(gates)
    chunks, pairs = gates // part_gates, dates // 2
    gate_rows, looks = total_gates // ML_RG, lanes // ML_AZ
    tables = focus_tables(shards, part_gates, lanes)
    tables.update(filter_tables(gate_rows, looks, dates))
    places, pack = packed(tables)
    rows = shards * part_gates
    block = (chunks, shards, 6 * (part_gates // ML_RG), lanes)
    columns = (chunks, pairs, shards, 4 * part_gates, lanes)
    return pl.pallas_call(
        functools.partial(stack_kernel, shards, places),
        in_specs=[pl.BlockSpec(memory_space=pl.ANY)] * 5,
        out_specs=VMEM,
        out_shape=jax.ShapeDtypeStruct((dates, 2, looks, gate_rows), jnp.float32),
        scratch_shapes=[
            pltpu.VMEM(pack.shape, pack.dtype),
            pltpu.VMEM(raw_echo.shape, raw_echo.dtype),
            pltpu.VMEM(range_filter.shape, range_filter.dtype),
            pltpu.VMEM(azimuth_phase.shape, azimuth_phase.dtype),
            pltpu.VMEM(columns, jnp.bfloat16),
            pltpu.VMEM(columns, jnp.bfloat16),
            pltpu.VMEM(azimuth_phase.shape[::-1], jnp.float32),
            pltpu.VMEM((chunks, 2, rows, lanes), jnp.float32),
            pltpu.VMEM((2 * shards, lanes), jnp.float32),
            pltpu.VMEM((2 * rows, 2 * lanes), jnp.float32),
            pltpu.VMEM((dates, rows, 2 * lanes), jnp.float32),
            pltpu.VMEM(block, jnp.bfloat16),
            pltpu.VMEM(block, jnp.bfloat16),
            pltpu.VMEM((dates, gate_rows, 2 * looks), jnp.float32),
            pltpu.VMEM((pairs, gate_rows, 2 * looks), jnp.float32),
            pltpu.SMEM(pair_offset.shape, pair_offset.dtype),
            pltpu.SemaphoreType.DMA((chunks * (pairs + 1),)),
            pltpu.SemaphoreType.DMA((chunks * (pairs + 1),)),
            pltpu.SemaphoreType.DMA((5,)),
            pltpu.SemaphoreType.REGULAR((3,)),
        ],
        compiler_params=pltpu.CompilerParams(collective_id=0, has_side_effects=True, vmem_limit_bytes=54784 * 1024),
        name="stack",
    )(pair_offset, raw_echo, range_filter, azimuth_phase, pack)


def tri_window():
    return 1.0 - np.abs(np.arange(PATCH) - (PATCH - 1) / 2.0) / HALF


def patch_maps(cells, starts):
    count = len(starts)
    forward = np.zeros((cells, count, PATCH), np.complex128)
    backward = np.zeros((count, PATCH, cells), np.complex128)
    window, k = tri_window(), np.arange(PATCH)
    for patch, start in enumerate(starts):
        for a in range(PATCH):
            cell = start + a
            if 0 <= cell < cells:
                wave = np.exp(2j * np.pi / PATCH * (k * a % PATCH))
                forward[cell, patch] = np.conj(wave)
                backward[patch, :, cell] = wave * window[a] / PATCH
    return forward.reshape(cells, -1), backward.reshape(-1, cells)


def filter_tables(gate_rows, looks, dates):
    gate_starts = range(-HALF, gate_rows - HALF + 1, HALF)
    line_starts = range(0, looks + 1, HALF)
    gate_fwd, gate_back = patch_maps(gate_rows, gate_starts)
    line_fwd, _ = patch_maps(looks + PATCH, line_starts)
    _, line_back = patch_maps(looks, [start - HALF for start in line_starts])
    width = (len(line_starts) - 1) * PATCH
    span = 2 * looks

    def entry(columns, main, low, table):
        block = right_block(columns).reshape(2, looks + PATCH, -1)
        for part in range(2):
            table[main + part * looks : main + (part + 1) * looks] += block[part, HALF : HALF + looks]
            at = low + part * 2 * HALF
            table[at : at + HALF] += block[part, :HALF]
            table[at + HALF : at + 2 * HALF] += block[part, HALF + looks :]

    enter = np.zeros((2, 2 * span, 2 * width))
    for parity in range(2):
        entry(line_fwd[:, :width], 0, span + parity * 4 * HALF, enter[parity])
    wide = dates * PATCH
    extra = np.zeros((dates * span + dates // 2 * span, 2 * wide))
    back = np.zeros((dates, 2 * looks, 2 * width + 2 * wide))
    for date in range(dates):
        placed = np.zeros((looks + PATCH, wide), np.complex128)
        placed[:, date * PATCH : (date + 1) * PATCH] = line_fwd[:, width:]
        entry(placed, date * span, dates * span + date // 2 * span + date % 2 * 4 * HALF, extra)
        placed = np.zeros((wide, looks), np.complex128)
        placed[date * PATCH : (date + 1) * PATCH] = line_back[width:]
        back[date, :, : 2 * width] = right_block(line_back[:width]).T
        back[date, :, 2 * width :] = right_block(placed).T
    gap = (np.arange(PATCH)[:, None] - np.arange(PATCH)[None, :]) % PATCH
    near = (gap <= 1) | (gap == PATCH - 1)
    group = max(2 * width, wide) // PATCH
    near_line = np.kron(np.eye(group), near)
    level = np.kron(np.eye(group), np.ones((PATCH, PATCH)) / PATCH**2)
    return {
        "enter": enter,
        "extra": extra,
        "gate_fwd": left_block(gate_fwd.T),
        "near_line": near_line,
        "level": level,
        "gate_back": left_block(gate_back.T),
        "line_back": back,
    }


def packed(tables):
    places, panels, first = {}, [], 0
    for name, table in tables.items():
        stack = table.reshape((-1,) + table.shape[-2:])
        _, height, width = stack.shape
        count = -(-width // LANES)
        places[name] = (first, height, count, width)
        for part in np.pad(stack, ((0, 0), (0, 0), (0, count * LANES - width))):
            for i in range(count):
                panels.append(part[:, i * LANES : (i + 1) * LANES])
                first += height
    return places, np.concatenate(panels).astype(ml_dtypes.bfloat16)


def body(raw_echo, range_filter, azimuth_phase, pair_offset):
    shards = lax.axis_size("lines")
    image = filtered_looks(raw_echo, range_filter, azimuth_phase, pair_offset, shards)
    return image.transpose(0, 1, 3, 2)


def solution(mesh):
    placed = (P("groups", None, "lines", None), P(), P("lines", None), P())
    return jax.shard_map(
        body,
        mesh=mesh,
        in_specs=placed,
        out_specs=P("groups", None, None, "lines"),
        check_vma=False,
    )
```

```python
import functools

import jax
import jax.numpy as jnp
import ml_dtypes
import numpy as np
from jax import lax
from jax.experimental import pallas as pl
from jax.experimental.pallas import tpu as pltpu
from jax.sharding import PartitionSpec as P

ML_RG = 4
ML_AZ = 2
PATCH = 32
HALF = PATCH // 2
BOX_FLOOR = 0.25
LANES = 128
VMEM = pl.BlockSpec(memory_space=pltpu.VMEM)


def right_block(table):
    return np.block([[table.real, table.imag], [-table.imag, table.real]])


def left_block(table):
    return np.block([[table.real, -table.imag], [table.imag, table.real]])


def split(value):
    high = value.astype(jnp.bfloat16)
    low = (value - high.astype(jnp.float32)).astype(jnp.bfloat16)
    return high, low


def mm(a, b):
    return jnp.dot(a, b, preferred_element_type=jnp.float32)


def exact_times(value, table):
    high, low = split(value)
    return mm(high, table) + mm(low, table)


def fft_leading(re, im, sign):
    count = len(re)
    if count == 1:
        return re, im
    if count == 2:
        return [re[0] + re[1], re[0] - re[1]], [im[0] + im[1], im[0] - im[1]]
    er, ei = fft_leading(re[0::2], im[0::2], sign)
    odr, odi = fft_leading(re[1::2], im[1::2], sign)
    half = count // 2
    out_r, out_i = [None] * count, [None] * count
    for k in range(half):
        angle = sign * 2.0 * np.pi * k / count
        c, s = float(np.cos(angle)), float(np.sin(angle))
        if k == 0:
            tr, ti = odr[k], odi[k]
        elif 4 * k == count:
            tr, ti = (-odi[k], odr[k]) if sign > 0 else (odi[k], -odr[k])
        else:
            tr = odr[k] * c - odi[k] * s
            ti = odr[k] * s + odi[k] * c
        out_r[k], out_i[k] = er[k] + tr, ei[k] + ti
        out_r[k + half], out_i[k + half] = er[k] - tr, ei[k] - ti
    return out_r, out_i


def weigh(spectra, table):
    rows, width = spectra.shape[0] // 2, spectra.shape[1]
    re, im = spectra[:rows], spectra[rows:]
    power = (re * re + im * im).astype(jnp.bfloat16)
    shape = (rows // PATCH, PATCH, width)
    near = mm(power, table("near_line")[:width, :width]).reshape(shape)
    level = jnp.sum(mm(power, table("level")[:width, :width]).reshape(shape), axis=1)
    scale = 1.0 / (9.0 * (level + 1e-06))
    weights = []
    for patch in range(rows // PATCH):
        value = near[patch]
        value = value + pltpu.roll(value, 1, 0) + pltpu.roll(value, PATCH - 1, 0)
        value = value * scale[patch : patch + 1] + BOX_FLOOR
        weights.append(value * lax.rsqrt(value))
    weight = jnp.concatenate(weights, axis=0)
    return jnp.concatenate([re * weight, im * weight], axis=0).astype(jnp.bfloat16)


def filter_dates(cells_ref, rims_ref, table, out_ref):
    dates, _, looks, gate_rows = out_ref.shape
    main = [cells_ref[date].astype(jnp.bfloat16) for date in range(dates)]
    rims = [rims_ref[pair].astype(jnp.bfloat16) for pair in range(dates // 2)]
    real, imag = [], []
    for date in range(dates):
        half = mm(jnp.concatenate([main[date], rims[date // 2]], axis=1), table("enter", date % 2)).astype(jnp.bfloat16)
        width = half.shape[1] // 2
        real.append(half[:, :width])
        imag.append(half[:, width:])
    half = mm(jnp.concatenate(main + rims, axis=1), table("extra")).astype(jnp.bfloat16)
    width = half.shape[1] // 2
    real.append(half[:, :width])
    imag.append(half[:, width:])
    groups = [(first, min(first + 2, dates + 1)) for first in range(0, dates + 1, 2)]
    spectra = []
    for first, last in groups:
        re, im = jnp.concatenate(real[first:last], axis=1), jnp.concatenate(imag[first:last], axis=1)
        spectra.append(mm(table("gate_fwd"), jnp.concatenate([re, im], axis=0)))
    weighted = [weigh(value, table) for value in spectra]
    image_re, image_im = [], []
    for (first, last), value in zip(groups, weighted):
        image = mm(table("gate_back"), value).astype(jnp.bfloat16)
        step = image.shape[1] // (last - first)
        for start in range(0, image.shape[1], step):
            image_re.append(image[:gate_rows, start : start + step])
            image_im.append(image[gate_rows:, start : start + step])
    contract = (((1,), (1,)), ((), ()))
    for date in range(dates):
        image = jnp.concatenate([image_re[date], image_im[date], image_re[dates], image_im[dates]], axis=1)
        result = lax.dot_general(table("line_back", date), image, contract, preferred_element_type=jnp.float32)
        out_ref[date, 0] = result[:looks]
        out_ref[date, 1] = result[looks:]


def chunk_gates(gates):
    return gates // 2 if gates % (2 * 4 * ML_RG) == 0 else gates


def stack_kernel(
    shards, places, offset_hbm, raw_hbm, filt_hbm, phase_hbm, pack_hbm, out_ref, pack, raw_ref, filt_ref, phase_ref,
    sent, columns, turned, trig, twid_ref, work, focused, looks_sent, looks_got, cells, rims, offset_ref, send_sem, recv_sem, load_sem, relay_sem,
):
    def table(name, index=0):
        first, height, panels, width = places[name]
        first += index * height * panels
        parts = [pack[first + i * height : first + (i + 1) * height, :] for i in range(panels)]
        whole = parts[0] if panels == 1 else jnp.concatenate(parts, axis=1)
        return whole[:, :width]

    dates, _, line_count, total_gates = raw_ref.shape
    chunks, pairs, _, block_rows, lanes = columns.shape
    gates = total_gates // shards
    part_gates = gates // chunks
    me = lax.axis_index("lines")

    loads = [
        pltpu.make_async_copy(source, target, load_sem.at[i])
        for i, (source, target) in enumerate(
            [(filt_hbm, filt_ref), (raw_hbm, raw_ref), (phase_hbm, phase_ref), (pack_hbm, pack), (offset_hbm, offset_ref)]
        )
    ]
    loads[0].start()
    loads[1].start()

    def ring(step):
        return lax.rem(me + step, shards)

    barrier = pltpu.get_barrier_semaphore()

    def signal(sem, peer):
        pl.semaphore_signal(sem, inc=1, device_id={"lines": peer}, device_id_type=pl.DeviceIdType.MESH)

    quarter = shards // 4
    mine = me // quarter
    @pl.loop(1, shards)
    def _(step):
        peer = ring(step)

        @pl.when(peer // quarter >= mine - 1)
        def _():
            signal(barrier, peer)


    def compress(chunk, pair):
        weights = filt_ref[...]
        if chunks > 1:
            weights = weights.reshape(2, shards, chunks, part_gates, total_gates)[:, :, chunk]
        weights = weights.reshape(2 * shards * part_gates, total_gates)
        half = shards * part_gates
        contract = (((1,), (1,)), ((), ()))
        for i in range(2):
            lines = raw_ref[2 * pair + i].reshape(2 * line_count, total_gates)
            product = lax.dot_general(weights, lines, contract, preferred_element_type=jnp.float32)
            real = product[:half, :line_count] - product[half:, line_count:]
            imag = product[half:, :line_count] + product[:half, line_count:]
            shape = (shards, part_gates, line_count)
            both = jnp.concatenate([real.reshape(shape), imag.reshape(shape)], axis=1)
            at = pl.ds(2 * i * part_gates, 2 * part_gates)
            sent[chunk, pair, :, at, :] = both.astype(jnp.bfloat16)

    def block(source, target, slot, peer):
        return pltpu.make_async_remote_copy(
            src_ref=source, dst_ref=target, send_sem=send_sem.at[slot], recv_sem=recv_sem.at[slot],
            device_id={"lines": peer}, device_id_type=pl.DeviceIdType.MESH,
        )

    def send_block(chunk, pair, peer):
        block(sent.at[chunk, pair, peer], columns.at[chunk, pair, me], chunk * pairs + pair, peer).start()

    def send_part(chunk, pair):
        @pl.loop(1, shards)
        def _(step):
            send_block(chunk, pair, ring(step))

        columns[chunk, pair, me] = sent[chunk, pair, me]

    half = shards // 2

    def send_looks(chunk, first, last):
        @pl.loop(first, last)
        def _(step):
            peer = lax.rem((me // half) * half + lax.rem(me + step, half) + (step // half) * half, shards)
            block(looks_sent.at[chunk, peer], looks_got.at[chunk, me], chunks * pairs + chunk, peer).start()

    def arrived(chunk, pair):
        part = pl.ds(0, shards - 1)
        slot = chunk * pairs + pair
        return block(sent.at[chunk, pair, part], columns.at[chunk, pair, part], slot, ring(1))

    def gathered(chunk):
        part = pl.ds(0, shards - 1)
        return block(looks_sent.at[chunk, part], looks_got.at[chunk, part], chunks * pairs + chunk, ring(1))

    loads[0].wait()
    loads[1].wait()
    for load in loads[2:]:
        load.start()
    for chunk in range(chunks):
        if chunk == 0:
            compress(0, 0)
            pl.semaphore_wait(barrier, jnp.minimum(mine + 2, 4) * quarter - 1)

            @pl.when((mine == 1) | (mine == 2))
            def _():
                signal(relay_sem.at[0], me - quarter)

            @pl.loop(1, shards)
            def _(step):
                peer = ring(step)

                @pl.when(peer // quarter <= mine + 1)
                def _():
                    send_block(0, 0, peer)

            @pl.when(mine < 2)
            def _():
                pl.semaphore_wait(relay_sem.at[0], 1)

                @pl.when(mine == 1)
                def _():
                    signal(relay_sem.at[1], me - quarter)

                @pl.loop(0, quarter)
                def _(step):
                    send_block(0, 0, (mine + 2) * quarter + step)

            @pl.loop(1, pairs)
            def _(pair):
                compress(0, pair)

            @pl.when(mine == 0)
            def _():
                pl.semaphore_wait(relay_sem.at[1], 1)

                @pl.loop(0, quarter)
                def _(step):
                    send_block(0, 0, 3 * quarter + step)

            columns[0, 0, me] = sent[0, 0, me]

            @pl.loop(1, pairs)
            def _(pair):
                send_part(0, pair)
        else:
            @pl.loop(0, pairs)
            def _(pair):
                compress(chunk, pair)
                send_part(chunk, pair)

    loads[2].wait()
    turned[...] = phase_ref[...].T

    @pl.loop(0, shards)
    def _(k):
        phase = turned[pl.ds(k, lanes, stride=shards), :].T
        at = pl.ds(pl.multiple_of(k * part_gates, part_gates), part_gates)
        cosine, sine = jnp.cos(phase), jnp.sin(phase)
        for chunk in range(chunks):
            trig[chunk, 0, at, :] = cosine[chunk * part_gates : (chunk + 1) * part_gates]
            trig[chunk, 1, at, :] = sine[chunk * part_gates : (chunk + 1) * part_gates]

    loads[3].wait()
    loads[4].wait()
    pieces = table("twiddle").astype(jnp.float32)
    count = twid_ref.shape[0]
    twid_ref[...] = pieces[:count] + pieces[count : 2 * count] + pieces[2 * count :]
    rows = shards * part_gates
    looks_rows = places["gate_sum"][1] // 3
    tile = looks_rows // shards

    @pl.loop(0, chunks)
    def _(chunk):
        @pl.loop(0, pairs)
        def _(pair):
            arrived(chunk, pair).wait_recv()

            @pl.when((chunk > 0) & (pair == pairs - 1))
            def _():
                send_looks(chunk - 1, half, shards)

            for i in range(2):
                start = 2 * i * part_gates
                data = [
                    columns[chunk, pair, s, pl.ds(start, 2 * part_gates), :].astype(jnp.float32) for s in range(shards)
                ]
                for low in range(0, part_gates, 8):
                    re = [value[low : low + 8] for value in data]
                    im = [value[part_gates + low : part_gates + low + 8] for value in data]
                    re, im = fft_leading(re, im, -1.0)
                    for k in range(shards):
                        c, s = twid_ref[pl.ds(k, 1), :], twid_ref[pl.ds(shards + k, 1), :]
                        at = pl.ds(i * rows + k * part_gates + low, 8)
                        work[at, :lanes] = re[k] * c + im[k] * s
                        work[at, lanes:] = im[k] * c - re[k] * s
            spectrum = mm(work[...].astype(jnp.bfloat16), table("forward"))
            c, s = trig[chunk, 0], trig[chunk, 1]
            shifted = []
            for i in range(2):
                re, im = spectrum[i * rows : (i + 1) * rows, :lanes], spectrum[i * rows : (i + 1) * rows, lanes:]
                shifted.append(jnp.concatenate([re * c - im * s, re * s + im * c], axis=1))
            work[...] = mm(jnp.concatenate(shifted, axis=0).astype(jnp.bfloat16), table("backward"))
            for i in range(2):
                for low in range(0, part_gates, 8):
                    re, im = [], []
                    for k in range(shards):
                        c, s = twid_ref[pl.ds(k, 1), :], twid_ref[pl.ds(shards + k, 1), :]
                        at = pl.ds(i * rows + k * part_gates + low, 8)
                        a, b = work[at, :lanes], work[at, lanes:]
                        re.append(a * c - b * s)
                        im.append(b * c + a * s)
                    re, im = fft_leading(re, im, 1.0)
                    for n in range(shards):
                        at = pl.ds(n * part_gates + low, 8)
                        focused[2 * pair + i, at, :lanes] = re[n].astype(jnp.bfloat16).astype(jnp.float32)
                        focused[2 * pair + i, at, lanes:] = im[n].astype(jnp.bfloat16).astype(jnp.float32)

        joined = []
        for parity in range(2):
            parts = []
            for d in (parity, parity + 2):
                partner = lax.rem(d + offset_ref[d], dates)
                a, b = focused[d, :, :lanes], focused[d, :, lanes:]
                p, q = focused[partner, :, :lanes], focused[partner, :, lanes:]
                parts.append(jnp.concatenate([a * p + b * q, b * p - a * q], axis=1).astype(jnp.bfloat16))
            joined.append(jnp.concatenate(parts, axis=0))
        summed = [mm(table("gate_sum"), value).astype(jnp.bfloat16) for value in joined]
        pieces = [mm(value[:looks_rows], table("main")) for value in summed]
        sides = [jnp.concatenate([value[looks_rows : 2 * looks_rows], value[2 * looks_rows :]], axis=1) for value in summed]
        rim = mm(sides[0], table("rim", 0)) + mm(sides[1], table("rim", 1))
        shaped = [piece.reshape(shards, tile, lanes) for piece in pieces + [rim]]
        looks_sent[chunk] = jnp.concatenate(shaped, axis=1).astype(looks_sent.dtype)

        looks_got[chunk, me] = looks_sent[chunk, me]

        @pl.when(chunk == chunks - 1)
        def _():
            send_looks(chunk, half, shards)

            @pl.loop(0, chunks)
            def _(earlier):
                send_looks(earlier, 1, half)

    @pl.loop(0, chunks)
    def _(chunk):
        @pl.loop(0, pairs)
        def _(pair):
            arrived(chunk, pair).wait_send()

    part_looks = tile // 2
    for chunk in range(chunks):
        gathered(chunk).wait_recv()
        for shard in range(shards):
            received = looks_got[chunk, shard].astype(jnp.float32)
            at = pl.ds((shard * chunks + chunk) * part_looks, part_looks)
            for q in range(2):
                for parity in range(2):
                    low = parity * tile + q * part_looks
                    cells[2 * q + parity, at, :] = received[low : low + part_looks]
                low = 2 * tile + q * part_looks
                rims[q, at, :] = received[low : low + part_looks]

    filter_dates(cells, rims, table, out_ref)

    @pl.loop(0, chunks)
    def _(chunk):
        gathered(chunk).wait_send()


def focus_tables(shards, part_gates, lanes):
    total = shards * lanes
    k1, n2 = np.arange(shards), np.arange(lanes)
    angle = 2.0 * np.pi / total * (np.outer(k1, n2) % total)
    twiddle = np.stack([np.cos(angle), np.sin(angle)]).astype(np.float32)
    grid = np.exp(-2j * np.pi / lanes * (np.outer(n2, n2) % lanes))
    forward = right_block(grid)
    backward = right_block(np.conj(grid)) / total
    group = np.kron(np.eye(part_gates // ML_RG), np.ones((1, ML_RG)))
    gate_sum = []
    for shift in (0, -1, 1):
        spread = np.einsum("js,qr,lg->jqlrsg", np.eye(shards, k=shift), np.eye(2), group)
        gate_sum.append(spread.reshape(shards * 2 * group.shape[0], -1))
    gate_sum = np.concatenate(gate_sum)
    looks = lanes // ML_AZ
    pair = np.kron(np.eye(looks), np.ones((ML_AZ, 1))) / (ML_RG * ML_AZ)
    main = np.kron(np.eye(2), pair)
    rim = np.zeros((2, 4 * lanes, lanes))
    for parity in range(2):
        for part in range(2):
            low = parity * 4 * HALF + part * 2 * HALF
            source = part * lanes
            rim[parity, source : source + lanes, low : low + HALF] = pair[:, looks - HALF :]
            source += 2 * lanes
            rim[parity, source : source + lanes, low + HALF : low + 2 * HALF] = pair[:, :HALF]
    twiddle = twiddle.reshape(2 * shards, lanes)
    high = twiddle.astype(ml_dtypes.bfloat16).astype(np.float32)
    middle = (twiddle - high).astype(ml_dtypes.bfloat16).astype(np.float32)
    pieces = np.concatenate([high, middle, twiddle - high - middle])
    return {
        "twiddle": pieces, "forward": forward, "backward": backward, "gate_sum": gate_sum, "main": main, "rim": rim,
    }


def filtered_looks(raw_echo, range_filter, azimuth_phase, pair_offset, shards):
    dates, _, lanes, total_gates = raw_echo.shape
    gates = azimuth_phase.shape[0]
    part_gates = chunk_gates(gates)
    chunks, pairs = gates // part_gates, dates // 2
    gate_rows, looks = total_gates // ML_RG, lanes // ML_AZ
    tables = focus_tables(shards, part_gates, lanes)
    tables.update(filter_tables(gate_rows, looks, dates))
    places, pack = packed(tables)
    rows = shards * part_gates
    block = (chunks, shards, 6 * (part_gates // ML_RG), lanes)
    columns = (chunks, pairs, shards, 4 * part_gates, lanes)
    return pl.pallas_call(
        functools.partial(stack_kernel, shards, places),
        in_specs=[pl.BlockSpec(memory_space=pl.ANY)] * 5,
        out_specs=VMEM,
        out_shape=jax.ShapeDtypeStruct((dates, 2, looks, gate_rows), jnp.float32),
        scratch_shapes=[
            pltpu.VMEM(pack.shape, pack.dtype),
            pltpu.VMEM(raw_echo.shape, raw_echo.dtype),
            pltpu.VMEM(range_filter.shape, range_filter.dtype),
            pltpu.VMEM(azimuth_phase.shape, azimuth_phase.dtype),
            pltpu.VMEM(columns, jnp.bfloat16),
            pltpu.VMEM(columns, jnp.bfloat16),
            pltpu.VMEM(azimuth_phase.shape[::-1], jnp.float32),
            pltpu.VMEM((chunks, 2, rows, lanes), jnp.float32),
            pltpu.VMEM((2 * shards, lanes), jnp.float32),
            pltpu.VMEM((2 * rows, 2 * lanes), jnp.float32),
            pltpu.VMEM((dates, rows, 2 * lanes), jnp.float32),
            pltpu.VMEM(block, jnp.bfloat16),
            pltpu.VMEM(block, jnp.bfloat16),
            pltpu.VMEM((dates, gate_rows, 2 * looks), jnp.float32),
            pltpu.VMEM((pairs, gate_rows, 2 * looks), jnp.float32),
            pltpu.SMEM(pair_offset.shape, pair_offset.dtype),
            pltpu.SemaphoreType.DMA((chunks * (pairs + 1),)),
            pltpu.SemaphoreType.DMA((chunks * (pairs + 1),)),
            pltpu.SemaphoreType.DMA((5,)),
            pltpu.SemaphoreType.REGULAR((2,)),
        ],
        compiler_params=pltpu.CompilerParams(collective_id=0, has_side_effects=True, vmem_limit_bytes=54784 * 1024),
        name="stack",
    )(pair_offset, raw_echo, range_filter, azimuth_phase, pack)


def tri_window():
    return 1.0 - np.abs(np.arange(PATCH) - (PATCH - 1) / 2.0) / HALF


def patch_maps(cells, starts):
    count = len(starts)
    forward = np.zeros((cells, count, PATCH), np.complex128)
    backward = np.zeros((count, PATCH, cells), np.complex128)
    window, k = tri_window(), np.arange(PATCH)
    for patch, start in enumerate(starts):
        for a in range(PATCH):
            cell = start + a
            if 0 <= cell < cells:
                wave = np.exp(2j * np.pi / PATCH * (k * a % PATCH))
                forward[cell, patch] = np.conj(wave)
                backward[patch, :, cell] = wave * window[a] / PATCH
    return forward.reshape(cells, -1), backward.reshape(-1, cells)


def filter_tables(gate_rows, looks, dates):
    gate_starts = range(-HALF, gate_rows - HALF + 1, HALF)
    line_starts = range(0, looks + 1, HALF)
    gate_fwd, gate_back = patch_maps(gate_rows, gate_starts)
    line_fwd, _ = patch_maps(looks + PATCH, line_starts)
    _, line_back = patch_maps(looks, [start - HALF for start in line_starts])
    width = (len(line_starts) - 1) * PATCH
    span = 2 * looks

    def entry(columns, main, low, table):
        block = right_block(columns).reshape(2, looks + PATCH, -1)
        for part in range(2):
            table[main + part * looks : main + (part + 1) * looks] += block[part, HALF : HALF + looks]
            at = low + part * 2 * HALF
            table[at : at + HALF] += block[part, :HALF]
            table[at + HALF : at + 2 * HALF] += block[part, HALF + looks :]

    enter = np.zeros((2, 2 * span, 2 * width))
    for parity in range(2):
        entry(line_fwd[:, :width], 0, span + parity * 4 * HALF, enter[parity])
    wide = dates * PATCH
    extra = np.zeros((dates * span + dates // 2 * span, 2 * wide))
    back = np.zeros((dates, 2 * looks, 2 * width + 2 * wide))
    for date in range(dates):
        placed = np.zeros((looks + PATCH, wide), np.complex128)
        placed[:, date * PATCH : (date + 1) * PATCH] = line_fwd[:, width:]
        entry(placed, date * span, dates * span + date // 2 * span + date % 2 * 4 * HALF, extra)
        placed = np.zeros((wide, looks), np.complex128)
        placed[date * PATCH : (date + 1) * PATCH] = line_back[width:]
        back[date, :, : 2 * width] = right_block(line_back[:width]).T
        back[date, :, 2 * width :] = right_block(placed).T
    gap = (np.arange(PATCH)[:, None] - np.arange(PATCH)[None, :]) % PATCH
    near = (gap <= 1) | (gap == PATCH - 1)
    group = max(2 * width, wide) // PATCH
    near_line = np.kron(np.eye(group), near)
    level = np.kron(np.eye(group), np.ones((PATCH, PATCH)) / PATCH**2)
    return {
        "enter": enter,
        "extra": extra,
        "gate_fwd": left_block(gate_fwd.T),
        "near_line": near_line,
        "level": level,
        "gate_back": left_block(gate_back.T),
        "line_back": back,
    }


def packed(tables):
    places, panels, first = {}, [], 0
    for name, table in tables.items():
        stack = table.reshape((-1,) + table.shape[-2:])
        _, height, width = stack.shape
        count = -(-width // LANES)
        places[name] = (first, height, count, width)
        for part in np.pad(stack, ((0, 0), (0, 0), (0, count * LANES - width))):
            for i in range(count):
                panels.append(part[:, i * LANES : (i + 1) * LANES])
                first += height
    return places, np.concatenate(panels).astype(ml_dtypes.bfloat16)


def body(raw_echo, range_filter, azimuth_phase, pair_offset):
    shards = lax.axis_size("lines")
    image = filtered_looks(raw_echo, range_filter, azimuth_phase, pair_offset, shards)
    return image.transpose(0, 1, 3, 2)


def solution(mesh):
    placed = (P("groups", None, "lines", None), P(), P("lines", None), P())
    return jax.shard_map(
        body,
        mesh=mesh,
        in_specs=placed,
        out_specs=P("groups", None, None, "lines"),
        check_vma=False,
    )
```
